32 devices in a mesh: grp: 2 (over y), tok: 8 (over z, core), head: 2 (over x).
Axes of the slice: x: 2, y: 2, z: 4, core: 2. Of those that a mesh axis runs over, the one named last changes fastest.
Arguments:
- queries: bfloat16 [2, 8192, 1280], P(None, ('grp', 'tok'), 'head'), parts along dimension 1, may hold values from -6 to 6
- key_tokens: bfloat16 [2, 8192, 1280], P(None, ('grp', 'tok'), 'head'), parts along dimension 1, may hold values from -6 to 6
- values: bfloat16 [2, 8192, 1280], P(None, ('grp', 'tok'), 'head'), parts along dimension 1, may hold values from -6 to 6
- learn_rates: float32 [2, 2, 8192], P(None, 'head', ('grp', 'tok')), parts along dimension 2, may hold values from 0.03 to 0.3
- w_first: float32 [2, 640, 640], P('head'), may hold values from -0.25 to 0.25
- w_second: float32 [2, 640, 640], P('head'), may hold values from -0.25 to 0.25
- w_third: float32 [2, 640, 640], P('head'), may hold values from -0.25 to 0.25
Outputs:
- layer_output: bfloat16 [2, 8192, 1280], P(None, ('grp', 'tok', 'head')), parts along dimension 1
The draws below stay inside these ranges and needn't reach their ends.
There are 2 independent parts, one for each index of `grp`. The reference program is written for one: setup_inputs(seed, part) draws one part's arguments, and reference() takes and returns one part's arrays. A program takes and returns all parts, laid end to end along the dimension named above; an argument that names none is the same for every part. Nothing has to cross between parts.
All inputs are finite; a program needn't handle non-finite values.
Results may differ from the reference program's by a relative error of at most 0.038.
Values may be sent and summed in bfloat16 or wider, within the bound.
No kernel may reach another device: no remote copies, remote signals or barrier semaphores. Data moves between devices by JAX's collectives and lax.ppermute only.
A program may use at most 64 MiB of HBM per device.

```python
import math
import jax
import jax.numpy as jnp
from jax import lax

HD = 640
F = 640
GROUPS = 2
HEADS = 2
GROUP_TOK = 4096


def levels(key, shape, cuts, least, largest):
    loudness = 1.0
    for dim, blocks in cuts:
        draws = jax.random.uniform(jax.random.fold_in(jax.random.fold_in(key, 6), dim), (blocks,), jnp.float32, least / len(cuts), largest / len(cuts))
        loudness = loudness * jnp.repeat(jnp.exp(draws), shape[dim] // blocks).reshape((-1,) + (1,) * (len(shape) - 1 - dim))
    return loudness


def gaussian(key, shape, width, most, split=(), held_as=jnp.bfloat16):
    entries = width * jax.random.normal(key, shape, jnp.float32)
    if split:
        entries = entries * levels(key, shape, split, -0.22, 0.18)
    return jnp.clip(entries, -most, most).astype(held_as)


def setup_inputs(seed: int = 0, part: int = 0) -> dict:
    key_list = jax.random.split(jax.random.key(seed), 8)
    own_keys = jax.random.split(jax.random.fold_in(key_list[7], part), 8)
    queries = gaussian(own_keys[0], (GROUPS, GROUP_TOK, HEADS * HD), 1.0, 6.0, ((1, 8), (2, 2)))
    key_tokens = gaussian(own_keys[1], (GROUPS, GROUP_TOK, HEADS * HD), 1.0, 6.0, ((1, 8), (2, 2)))
    values = gaussian(own_keys[2], (GROUPS, GROUP_TOK, HEADS * HD), 1.0, 6.0, ((1, 8), (2, 2)))
    learn_rates = jnp.clip(jnp.exp(math.log(0.3) - 2.3025852 * jax.random.uniform(own_keys[3], (GROUPS, HEADS, GROUP_TOK), jnp.float32) ** levels(own_keys[3], (GROUPS, HEADS, GROUP_TOK), ((1, 2), (2, 8)), -0.2, 0.2)), 0.03, 0.3)
    w_first = gaussian(key_list[4], (HEADS, F, HD), HD ** -0.5, 0.25, ((0, 2),), jnp.float32)
    w_second = gaussian(key_list[5], (HEADS, HD, F), F ** -0.5, 0.25, ((0, 2),), jnp.float32)
    w_third = gaussian(key_list[6], (HEADS, F, HD), HD ** -0.5, 0.25, ((0, 2),), jnp.float32)
    return {"queries": queries, "key_tokens": key_tokens, "values": values, "learn_rates": learn_rates, "w_first": w_first, "w_second": w_second, "w_third": w_third}


MOMENTUM_DECAY = 0.9
EPSILON = 1e-06
CONTRACT_ROWS = (((0,), (0,)), ((), ()))
CONTRACT_LAST = (((1,), (1,)), ((), ()))

def silu_slope(pre_act):
    sigmoid_value = jax.nn.sigmoid(pre_act)
    return sigmoid_value * (1.0 + pre_act * (1.0 - sigmoid_value))

def row_rms(matrix):
    return jnp.sqrt(lax.optimization_barrier(jnp.mean(matrix * matrix, axis=-1, keepdims=True)) + EPSILON)

def block_terms(keys_now, values_now, rates_now, first_b, second_b, third_b):
    pre_gate = lax.dot_general(keys_now, first_b, CONTRACT_LAST, preferred_element_type=jnp.float32)
    pre_up = lax.dot_general(keys_now, third_b, CONTRACT_LAST, preferred_element_type=jnp.float32)
    hidden = (jax.nn.silu(pre_gate) * pre_up).astype(jnp.bfloat16)
    scaled = (rates_now[:, None] * values_now.astype(jnp.float32)).astype(jnp.bfloat16)
    back_prop = jnp.dot(scaled, second_b, preferred_element_type=jnp.float32)
    grad_gate = (back_prop * pre_up * silu_slope(pre_gate)).astype(jnp.bfloat16)
    grad_up = (back_prop * jax.nn.silu(pre_gate)).astype(jnp.bfloat16)
    return (hidden, scaled, grad_gate, grad_up)

def weight_grads(gate_part, scaled_part, up_part, keys_now, hidden):
    grad_first = lax.dot_general(gate_part, keys_now, CONTRACT_ROWS, preferred_element_type=jnp.float32)
    grad_second = lax.dot_general(scaled_part, hidden, CONTRACT_ROWS, preferred_element_type=jnp.float32)
    grad_third = lax.dot_general(up_part, keys_now, CONTRACT_ROWS, preferred_element_type=jnp.float32)
    return (grad_first, grad_second, grad_third)

def apply_weights(queries_now, first_b, second_b, third_b):
    pre_gate = lax.dot_general(queries_now, first_b, CONTRACT_LAST, preferred_element_type=jnp.float32)
    pre_up = lax.dot_general(queries_now, third_b, CONTRACT_LAST, preferred_element_type=jnp.float32)
    hidden = (jax.nn.silu(pre_gate) * pre_up).astype(jnp.bfloat16)
    return lax.dot_general(hidden, second_b, CONTRACT_LAST, preferred_element_type=jnp.float32).astype(jnp.bfloat16)

def one_head(head_queries, head_keys, head_values, head_rates, first, second, third):
    current = [first, second, third]
    targets = [row_rms(matrix) for matrix in current]
    moment = [jnp.zeros_like(matrix) for matrix in current]
    grad_scale = 1.0 / math.sqrt(GROUP_TOK)
    rounded = [matrix.astype(jnp.bfloat16) for matrix in current]
    produced = []
    for block_index in range(GROUPS):
        keys_now = head_keys[block_index]
        hidden, scaled, grad_gate, grad_up = block_terms(keys_now, head_values[block_index], head_rates[block_index], rounded[0], rounded[1], rounded[2])
        grads = weight_grads(grad_gate, scaled, grad_up, keys_now, hidden)
        for index in range(3):
            moment[index] = MOMENTUM_DECAY * moment[index] + grads[index] * grad_scale
            summed = current[index] + moment[index]
            current[index] = summed * targets[index] / row_rms(summed)
        rounded = [matrix.astype(jnp.bfloat16) for matrix in current]
        produced.append(apply_weights(head_queries[block_index], rounded[0], rounded[1], rounded[2]))
    return jnp.stack(produced)

def reference(queries, key_tokens, values, learn_rates, w_first, w_second, w_third):
    head_outputs = []
    for head_index in range(HEADS):
        head_cols = slice(head_index * HD, (head_index + 1) * HD)
        head_outputs.append(one_head(queries[:, :, head_cols], key_tokens[:, :, head_cols], values[:, :, head_cols], learn_rates[:, head_index], w_first[head_index], w_second[head_index], w_third[head_index]))
    return jnp.concatenate(head_outputs, axis=2)
```

```python
import functools
import math

import jax
import jax.numpy as jnp
from jax import lax
from jax.experimental import pallas as pl
from jax.experimental.pallas import tpu as pltpu
from jax.sharding import PartitionSpec as P

DECAY = 0.9
EPS = 1e-06
F32 = jnp.float32
BF16 = jnp.bfloat16
NT = (((1,), (1,)), ((), ()))
NN = (((1,), (0,)), ((), ()))
PARTS = 4
GRANT = 16 * 2**20
VMEM = pl.BlockSpec(memory_space=pltpu.VMEM)
SMEM = pl.BlockSpec(memory_space=pltpu.SMEM)


def dot_nt(a, b):
    return lax.dot_general(a, b, NT, preferred_element_type=F32)


def dot_nn(a, b):
    return lax.dot_general(a, b, NN, preferred_element_type=F32)


def call(body, flags, operands, outs, flops=0):
    shapes = [jax.ShapeDtypeStruct(s, d) for s, d in outs]
    moved = sum(math.prod(o.shape) * o.dtype.itemsize for o in list(operands) + shapes)
    return pl.pallas_call(
        body,
        out_shape=shapes,
        in_specs=[SMEM] + [VMEM] * len(operands),
        out_specs=[VMEM] * len(shapes),
        compiler_params=pltpu.CompilerParams(vmem_limit_bytes=GRANT),
        cost_estimate=pl.CostEstimate(
            flops=int(flops), bytes_accessed=int(moved), transcendentals=0
        ),
    )(flags, *operands)


def silu_parts(gate):
    sig = jax.nn.sigmoid(gate)
    return sig, gate * sig


def row_scale(before, after):
    target = jnp.sqrt(jnp.mean(before * before, axis=-1, keepdims=True) + EPS)
    return target / jnp.sqrt(jnp.mean(after * after, axis=-1, keepdims=True) + EPS)


def prep_body(rows, flags, w1, w2, w3, u13, w2t, u2t, t2):
    base = pl.multiple_of(flags[0] * rows, 8)
    part = rows // PARTS
    for j in range(PARTS):
        at = pl.multiple_of(base + j * part, 8)
        u13[j, :part] = w1[0, pl.ds(at, part), :].astype(BF16)
        u13[j, part:] = w3[0, pl.ds(at, part), :].astype(BF16)
    w2sq = w2[0]
    flipped = w2sq.T
    w2t[...] = flipped
    t2[...] = jnp.sqrt(jnp.mean(flipped * flipped, axis=0, keepdims=True) + EPS)
    u2t[...] = w2t[pl.ds(base, rows), :].astype(BF16)


def first_body(last, scale, rows, flags, keys, scaled, u13, *refs):
    if last:
        partial, gate_up, g0, g1 = refs
    else:
        gate_up, partial = refs
    part = rows // PARTS
    kept = keys[0]
    rhs = scaled[...]
    for j in range(PARTS):
        both = dot_nt(u13[j], kept)
        gate_up[j] = both
        _, act = silu_parts(both[:part])
        hidden = (act * both[part:]).astype(BF16)
        grad = dot_nn(hidden, rhs)
        at = slice(j * part, (j + 1) * part)
        if last:
            total = ((grad + partial[at]) * scale).astype(BF16)
            dest = g0 if j < PARTS // 2 else g1
            off = (j % (PARTS // 2)) * part
            dest[off : off + part] = total
        else:
            partial[at] = grad


def second_body(scale, rows, flags, gu_own, gu_oth, u2t, k_own, k_oth, e_own, e_oth, *refs):
    stacks = refs[PARTS]
    part = rows // PARTS
    tokens = e_own.shape[0]
    for side, (gu, scaled) in enumerate(((gu_own, e_own), (gu_oth, e_oth))):
        cols = slice(side * tokens, (side + 1) * tokens)
        back = dot_nt(u2t[...], scaled[...])
        for j in range(PARTS):
            gate, up = gu[j, :part], gu[j, part:]
            d = back[j * part : (j + 1) * part]
            sig, act = silu_parts(gate)
            stacks[j, :part, cols] = (d * up * sig * (1.0 + gate * (1.0 - sig))).astype(BF16)
            stacks[j, part:, cols] = (d * act).astype(BF16)
    for j in range(PARTS):
        grad = dot_nn(stacks[j, :, :tokens], k_own[0]) + dot_nn(stacks[j, :, tokens:], k_oth[0])
        refs[j][...] = (grad * scale).astype(BF16)


def grad_body(j, scale, block, flags, new13, u2t, k_own, k_oth, e_own, e_oth, g13, g2):
    part = new13.shape[0] // 2
    w13 = new13[...]
    w2 = u2t[j * part : (j + 1) * part]
    sum13 = sum2 = None
    for keys, scaled in ((k_own, e_own), (k_oth, e_oth)):
        kept, rhs = keys[block], scaled[...]
        both = dot_nt(w13, kept)
        d = dot_nt(w2, rhs)
        gate, up = both[:part], both[part:]
        sig, act = silu_parts(gate)
        hidden = (act * up).astype(BF16)
        stack = jnp.concatenate(
            [d * up * sig * (1.0 + gate * (1.0 - sig)), d * act], axis=0
        ).astype(BF16)
        a, b = dot_nn(stack, kept), dot_nn(hidden, rhs)
        sum13 = a if sum13 is None else sum13 + a
        sum2 = b if sum2 is None else sum2 + b
    g13[...] = (sum13 * scale).astype(BF16)
    g2[...] = (sum2 * scale).astype(BF16)


def add_body(n_grad, has_prev, flags, *refs):
    refs = list(refs)
    rcv = refs.pop(0)
    grads = [refs.pop(0) for _ in range(n_grad)]
    prev = refs.pop(0) if has_prev else None
    if n_grad:
        out = refs.pop(0)
        off = 0
        for g in grads:
            n = g.shape[0]
            out[off : off + n] = (
                rcv[off : off + n].astype(F32) + g[...].astype(F32)
            ).astype(BF16)
            off += n
    if has_prev:
        out = refs.pop(0)
        outer = flags[1] != 0
        out[...] = jnp.where(outer, rcv[...], prev[...])


def sel_body(n_grad, flags, *refs):
    prev, out = refs[n_grad], refs[n_grad + 1]
    outer = flags[1] != 0
    off = 0
    for g in refs[:n_grad]:
        n = g.shape[0]
        out[off : off + n] = jnp.where(outer, g[...], prev[off : off + n])
        off += n


def upd13_first(j, rows, flags, s, m, w1, w3, u, w_new, moment):
    part = rows // PARTS
    at = pl.multiple_of(flags[0] * rows + j * part, 8)
    total = s[...].astype(F32) + m[...].astype(F32)
    moment[...] = total
    for i, w in enumerate((w1, w3)):
        sl = slice(i * part, (i + 1) * part)
        old = w[0, pl.ds(at, part), :]
        new = old + total[sl]
        new = new * row_scale(old, new)
        w_new[sl] = new
        u[sl] = new.astype(BF16)


def upd13_next(j, rows, flags, s, m, w1, w3, w_old, moment, u):
    part = rows // PARTS
    at = pl.multiple_of(flags[0] * rows + j * part, 8)
    new = w_old[...] + DECAY * moment[...] + (s[...].astype(F32) + m[...].astype(F32))
    for i, w in enumerate((w1, w3)):
        sl = slice(i * part, (i + 1) * part)
        u[sl] = (new[sl] * row_scale(w[0, pl.ds(at, part), :], new[sl])).astype(BF16)


def upd2_first(j, rows, flags, s, m, w2t, u, raw, moment):
    half = rows // 2
    at = pl.multiple_of(flags[0] * rows + j * half, 8)
    total = s[...].astype(F32) + m[...].astype(F32)
    new = w2t[pl.ds(at, half), :] + total
    moment[...] = total
    raw[...] = new
    u[...] = new.astype(BF16)


def upd2_next(flags, s, m, raw, moment, colscale, u):
    total = s[...].astype(F32) + m[...].astype(F32)
    u[...] = (raw[...] * colscale[...] + DECAY * moment[...] + total).astype(BF16)


def column_scale(pieces, t2):
    sq = None
    count = 0
    for p in pieces:
        v = p[...].astype(F32)
        q = jnp.sum(v * v, axis=0, keepdims=True)
        sq = q if sq is None else sq + q
        count += p.shape[0]
    return t2[...] / jnp.sqrt(sq / count + EPS)


def scale_body(n_own, flags, *refs):
    pieces, t2, colscale, outs = refs[:-4], refs[-4], refs[-3], refs[-2:]
    sc = column_scale(pieces, t2)
    colscale[...] = sc
    for side in range(2):
        off = 0
        for p in pieces[side * n_own : (side + 1) * n_own]:
            n = p.shape[0]
            outs[side][off : off + n] = (p[...].astype(F32) * sc).astype(BF16)
            off += n


def hidden_body(block, flags, queries, *refs):
    pieces, hidden, gate_rows, up_rows = refs[:-3], refs[-3], refs[-2], refs[-1]
    part = pieces[0].shape[0] // 2
    for i, p in enumerate(pieces):
        gate_rows[i * part : (i + 1) * part] = p[:part]
        up_rows[i * part : (i + 1) * part] = p[part:]
    q = queries[block]
    gate = dot_nt(q, gate_rows[...])
    up = dot_nt(q, up_rows[...])
    _, act = silu_parts(gate)
    hidden[...] = (act * up).astype(BF16)


def out_body(scaled, n_piece, flags, hidden, *refs):
    pieces, rest = refs[:n_piece], list(refs[n_piece:])
    t2 = rest.pop(0) if scaled else None
    out, stack = rest
    off = 0
    for p in pieces:
        n = p.shape[0]
        stack[off : off + n] = p[...]
        off += n
    n = out.shape[0]
    lhs = hidden[pl.ds(pl.multiple_of(flags[0] * n, 8), n), :]
    res = dot_nn(lhs, stack[...])
    if scaled:
        res = res * column_scale(pieces, t2)
    out[...] = res.astype(BF16)


def fin_body(flags, own0, oth0, own1, oth1, out):
    width = own0.shape[1]
    mine = pl.multiple_of(flags[2] * width, 128)
    other = pl.multiple_of((1 - flags[2]) * width, 128)
    for b, (own, oth) in enumerate(((own0, oth0), (own1, oth1))):
        out[b, :, pl.ds(mine, width)] = own[...]
        out[b, :, pl.ds(other, width)] = oth[...]


def local(queries, key_tokens, values, learn_rates, w_first, w_second, w_third):
    tok = lax.axis_size("tok")
    heads = lax.axis_size("head")
    tok_i = lax.axis_index("tok")
    head_i = lax.axis_index("head")
    cores = 2
    chips = tok // cores
    tokens, width = key_tokens.shape[1], key_tokens.shape[2]
    inner = w_first.shape[1]
    rows = inner // cores
    part = rows // PARTS
    half = rows // 2
    chunk = (half, width)
    grad_scale = 1.0 / math.sqrt(tokens * tok)
    lined = chips == 4
    chip_i = tok_i // cores
    outer = (chip_i == 0) | (chip_i == chips - 1) if lined else chip_i < 0
    flags = jnp.stack([tok_i % cores, outer.astype(jnp.int32), head_i]).astype(jnp.int32)

    def shift(x, pairs):
        return lax.ppermute(x, "tok", pairs)

    def chip_pairs(to):
        return [(c * cores + i, to[c] * cores + i) for c in range(chips) for i in range(cores)]

    core_pairs = [(i, i ^ 1) for i in range(tok)]
    swap_ends = chip_pairs([1, 0, 3, 2]) if lined else None
    swap_mid = chip_pairs([0, 2, 1, 3]) if lined else None

    k_oth = shift(key_tokens, core_pairs)
    rates = learn_rates[:, 0, :, None]
    e_own, e_oth = [], []
    for b in range(2):
        e = (rates[b] * values[b].astype(F32)).astype(BF16)
        e_own.append(e)
        e_oth.append(shift(e, core_pairs))

    full = (inner, width)
    u13, w2t, u2t, t2 = call(
        functools.partial(prep_body, rows),
        flags,
        (w_first, w_second, w_third),
        [((PARTS, half, width), BF16), (full, F32), ((rows, width), BF16), ((1, width), F32)],
    )
    gu_shape = ((PARTS, half, tokens), F32)
    mm = 2 * rows * width * tokens
    gu_own, partial = call(
        functools.partial(first_body, False, grad_scale, rows),
        flags,
        (key_tokens, e_own[0], u13),
        [gu_shape, ((rows, width), F32)],
        3 * mm,
    )
    gu_oth, g0, g1 = call(
        functools.partial(first_body, True, grad_scale, rows),
        flags,
        (k_oth, e_oth[0], u13, partial),
        [gu_shape, (chunk, BF16), (chunk, BF16)],
        3 * mm,
    )
    *g_rest, _ = call(
        functools.partial(second_body, grad_scale, rows),
        flags,
        (gu_own, gu_oth, u2t, key_tokens, k_oth, e_own[0], e_oth[0]),
        [(chunk, BF16)] * PARTS + [((PARTS, half, 2 * tokens), BF16)],
        6 * mm,
    )
    total = 2 * (PARTS + 2)
    grads = {0: [g0], 1: [g1]}
    for j in range(PARTS):
        grads[2 + j] = [g_rest[j]]
    weights, finals, others = {}, {}, {}
    state = {}
    first13, next13, next2 = 2, PARTS + 2, 2 * PARTS + 2

    def update(k, s, m):
        b16, f32 = (chunk, BF16), (chunk, F32)
        if k < first13:
            u, raw, mom = call(
                functools.partial(upd2_first, k, rows), flags, (s, m, w2t), [b16, f32, f32]
            )
            state["w2", k] = (raw, mom)
        elif k < next13:
            j = k - first13
            u, new, mom = call(
                functools.partial(upd13_first, j, rows),
                flags,
                (s, m, w_first, w_third),
                [b16, f32, f32],
            )
            state["w13", j] = (new, mom)
        elif k < next2:
            j = k - next13
            (u,) = call(
                functools.partial(upd13_next, j, rows),
                flags,
                (s, m, w_first, w_third, *state["w13", j]),
                [b16],
            )
        else:
            (u,) = call(upd2_next, flags, (s, m, *state["w2", k - next2], state["scale"]), [b16])
        return u

    def arrived(k):
        others[k] = shift(finals[k], core_pairs)
        if k == 1:
            state["scale"], state["u2_own"], state["u2_oth"] = call(
                functools.partial(scale_body, 2),
                flags,
                (finals[0], finals[1], others[0], others[1], t2),
                [((1, width), F32), ((rows, width), BF16), ((rows, width), BF16)],
            )
        if first13 <= k < next13:
            j = k - first13
            g13, g2 = call(
                functools.partial(grad_body, j, grad_scale, 1),
                flags,
                (finals[k], state["u2_own"], key_tokens, k_oth, e_own[1], e_oth[1]),
                [(chunk, BF16), ((part, width), BF16)],
                12 * mm // PARTS,
            )
            grads[next13 + j] = [g13]
            grads.setdefault(next2 + j // 2, []).append(g2)

    def produce(b, first, second, t2_in):
        pieces = [finals[k] for k in first] + [others[k] for k in first]
        hidden, *_ = call(
            functools.partial(hidden_body, b),
            flags,
            (queries, *pieces),
            [((tokens, inner), BF16), (full, BF16), (full, BF16)],
            8 * mm,
        )
        scaled = t2_in is not None
        extra = (t2_in,) if scaled else ()

        def rows_of(which, n):
            res, _ = call(
                functools.partial(out_body, scaled, len(second)),
                which,
                (hidden, *second, *extra),
                [((n, width), BF16), (full, BF16)],
                4 * mm * n // tokens,
            )
            return res

        if heads != 2:
            whole = rows_of(jnp.zeros((1,), jnp.int32), tokens)
            return lax.all_to_all(whole, "head", split_axis=0, concat_axis=1, tiled=True)
        n = tokens // 2
        away = rows_of((1 - flags[2:]), n)
        came = lax.ppermute(away, "head", [(0, 1), (1, 0)])
        return rows_of(flags[2:], n), came

    def block0():
        return produce(
            0, range(first13, next13), (state["u2_own"], state["u2_oth"]), None
        )

    def block1():
        second = [finals[next2], finals[next2 + 1], others[next2], others[next2 + 1]]
        return produce(1, range(next13, next2), second, t2)

    if lined:
        plan = [
            (0, None), (1, None), (2, None), (3, 0), (4, 1), (5, 2), (None, 3), (6, 4),
            (7, 5), (8, None), (9, 6), (10, 7), (11, 8), (None, 9), (None, 10), (None, 11),
        ]
        flight = {}
        for inw, out in plan:
            if inw is not None and out is not None:
                g = grads[inw]
                (send,) = call(
                    functools.partial(sel_body, len(g)), flags, (*g, weights[out]), [(chunk, BF16)]
                )
            else:
                send = grads[inw][0] if inw is not None else weights[out]
                if inw is not None and len(grads[inw]) > 1:
                    send = jnp.concatenate(grads[inw], axis=0)
            rcv = shift(send, swap_ends)
            g = grads[inw] if inw is not None else []
            prev = (weights[out],) if out is not None else ()
            res = call(
                functools.partial(add_body, len(g), bool(prev)),
                flags,
                (rcv, *g, *prev),
                [(chunk, BF16)] * (bool(g) + len(prev)),
            )
            if inw is not None:
                met = shift(res[0], swap_mid)
                weights[inw] = update(inw, res[0], met)
            if out is not None:
                finals[out] = res[-1]
                arrived(out)
        del flight
    else:
        groups = [[c * cores + i for c in range(chips)] for i in range(cores)]
        zero = jnp.zeros(chunk, BF16)
        for k in range(total):
            g = grads[k][0] if len(grads[k]) == 1 else jnp.concatenate(grads[k], axis=0)
            s = lax.psum(g, "tok", axis_index_groups=groups)
            finals[k] = update(k, s, zero)
            arrived(k)
    if heads != 2:
        return jnp.stack([block0(), block1()])
    own0, came0 = block0()
    own1, came1 = block1()
    n = tokens // 2
    (out,) = call(fin_body, flags, (own0, came0, own1, came1), [((2, n, 2 * width), BF16)])
    return out


def solution(mesh):
    placed = (
        P(None, ("grp", "tok"), "head"),
        P(None, ("grp", "tok"), "head"),
        P(None, ("grp", "tok"), "head"),
        P(None, "head", ("grp", "tok")),
        P("head", None, None),
        P("head", None, None),
        P("head", None, None),
    )
    return jax.shard_map(
        local,
        mesh=mesh,
        in_specs=placed,
        out_specs=P(None, ("grp", "tok", "head"), None),
        check_vma=False,
    )
```

```python
import functools
import math

import jax
import jax.numpy as jnp
from jax import lax
from jax.experimental import pallas as pl
from jax.experimental.pallas import tpu as pltpu
from jax.sharding import PartitionSpec as P


DECAY = 0.9
EPS = 1e-06
F32 = jnp.float32
BF16 = jnp.bfloat16
NT = (((1,), (1,)), ((), ()))
NN = (((1,), (0,)), ((), ()))
PARTS = 4
GRANT = 16 * 2**20
VMEM = pl.BlockSpec(memory_space=pltpu.VMEM)
SMEM = pl.BlockSpec(memory_space=pltpu.SMEM)
HBM = pl.BlockSpec(memory_space=pltpu.HBM)


def dot_nt(a, b):
    return lax.dot_general(a, b, NT, preferred_element_type=F32)


def dot_nn(a, b):
    return lax.dot_general(a, b, NN, preferred_element_type=F32)


def call(body, flags, operands, outs, flops=0, hbm=(), out_hbm=False, sems=0, alias=None):
    shapes = [jax.ShapeDtypeStruct(s, d) for s, d in outs]
    moved = sum(math.prod(o.shape) * o.dtype.itemsize for o in list(operands) + shapes)
    return pl.pallas_call(
        body,
        out_shape=shapes,
        in_specs=[SMEM] + [HBM if i in hbm else VMEM for i in range(len(operands))],
        out_specs=[HBM if out_hbm else VMEM] * len(shapes),
        scratch_shapes=[pltpu.SemaphoreType.DMA((sems,))] if sems else [],
        input_output_aliases=alias or {},
        compiler_params=pltpu.CompilerParams(vmem_limit_bytes=GRANT),
        cost_estimate=pl.CostEstimate(
            flops=int(flops), bytes_accessed=int(moved), transcendentals=0
        ),
    )(flags, *operands)


def copies(sems, *pairs):
    started = [pltpu.make_async_copy(src, dst, sems.at[i]) for i, (src, dst) in enumerate(pairs)]
    for c in started:
        c.start()
    return started


def load_body(block, flags, keys, vals, k_out, v_out, sems):
    for c in copies(sems, (keys.at[block], k_out), (vals.at[block], v_out)):
        c.wait()


def silu_parts(gate):
    sig = jax.nn.sigmoid(gate)
    return sig, gate * sig


def row_scale(before, after):
    target = jnp.sqrt(jnp.mean(before * before, axis=-1, keepdims=True) + EPS)
    return target / jnp.sqrt(jnp.mean(after * after, axis=-1, keepdims=True) + EPS)


def first_body(last, scale, rows, flags, keys, vals, rates, *refs):
    if last:
        u13, partial, gate_up, g0, g1 = refs
    else:
        w1, w3, u13, w13, gate_up, partial, sems = refs
        at = pl.multiple_of(flags[0] * rows, 8)
        started = copies(
            sems,
            (w1.at[0, pl.ds(at, rows)], w13.at[pl.ds(0, rows)]),
            (w3.at[0, pl.ds(at, rows)], w13.at[pl.ds(rows, rows)]),
        )
        for c in started:
            c.wait()
        u13[...] = w13[...].astype(BF16)
    both = dot_nt(u13[...], keys[...])
    gate_up[...] = both
    _, act = silu_parts(both[:rows])
    hidden = (act * both[rows:] * rates[0]).astype(BF16)
    grad = dot_nn(hidden, vals[...])
    if last:
        total = ((grad + partial[...]) * scale).astype(BF16)
        g0[...] = total[: rows // 2]
        g1[...] = total[rows // 2 :]
    else:
        partial[...] = grad


def flip_body(rows, flags, w2, w2t, u2t, t2):
    flipped = w2[0].T
    w2t[...] = flipped
    t2[...] = jnp.sqrt(jnp.mean(flipped * flipped, axis=0, keepdims=True) + EPS)
    base = pl.multiple_of(flags[0] * rows, 8)
    u2t[...] = w2t[pl.ds(base, rows), :].astype(BF16)


def slopes(both, back, part):
    gate, up = both[:part], both[part:]
    sig, act = silu_parts(gate)
    stack = jnp.concatenate(
        [back * up * sig * (1.0 + gate * (1.0 - sig)), back * act], axis=0
    ).astype(BF16)
    return stack, act * up


def second_body(scale, rows, flags, gu_own, gu_oth, u2t, k_own, k_oth, v_own, v_oth, r_own, r_oth, *outs):
    grad = None
    for gu, keys, vals, rates in ((gu_own, k_own, v_own, r_own), (gu_oth, k_oth, v_oth, r_oth)):
        back = dot_nt(u2t[...], vals[...]) * rates[0]
        stack, _ = slopes(gu[...], back, rows)
        one = dot_nn(stack, keys[...])
        grad = one if grad is None else grad + one
    grad = (grad * scale).astype(BF16)
    part = rows // PARTS
    for j, out in enumerate(outs):
        out[:part] = grad[j * part : (j + 1) * part]
        out[part:] = grad[rows + j * part : rows + (j + 1) * part]


def grad_body(j, scale, block, flags, new13, u2t, k_own, k_oth, v_own, v_oth, r_own, r_oth, g13, g2):
    part = new13.shape[0] // 2
    w13 = new13[...]
    w2 = u2t[j * part : (j + 1) * part]
    sum13 = sum2 = None
    for keys, vals, rates in ((k_own, v_own, r_own), (k_oth, v_oth, r_oth)):
        kept, rhs = keys[...], vals[...]
        both = dot_nt(w13, kept)
        back = dot_nt(w2, rhs) * rates[block]
        stack, hidden = slopes(both, back, part)
        a = dot_nn(stack, kept)
        b = dot_nn((hidden * rates[block]).astype(BF16), rhs)
        sum13 = a if sum13 is None else sum13 + a
        sum2 = b if sum2 is None else sum2 + b
    g13[...] = (sum13 * scale).astype(BF16)
    g2[...] = (sum2 * scale).astype(BF16)


def emit(flags, out, at, new, grads):
    n = new.shape[0]
    off = 0
    for g in grads:
        lo, hi = max(at, off), min(at + n, off + g.shape[0])
        if lo < hi:
            out[lo:hi] = jnp.where(
                flags[1] != 0, g[lo - off : hi - off], new[lo - at : hi - at]
            )
        off += g.shape[0]
    if not grads:
        out[at : at + n] = new


def upd13_first(j, rows, flags, s, m, w13, *refs):
    *grads, send, w_new, moment = refs
    part = rows // PARTS
    total = s[...].astype(F32) + m[...].astype(F32)
    moment[...] = total
    for i in range(2):
        sl = slice(i * part, (i + 1) * part)
        old = w13[i * rows + j * part : i * rows + (j + 1) * part]
        new = old + total[sl]
        new = new * row_scale(old, new)
        w_new[sl] = new
        emit(flags, send, i * part, new.astype(BF16), grads)


def upd13_next(j, rows, flags, s, m, w13, w_old, moment, *refs):
    *grads, send = refs
    part = rows // PARTS
    new = w_old[...] + DECAY * moment[...] + (s[...].astype(F32) + m[...].astype(F32))
    for i in range(2):
        sl = slice(i * part, (i + 1) * part)
        old = w13[i * rows + j * part : i * rows + (j + 1) * part]
        emit(flags, send, i * part, (new[sl] * row_scale(old, new[sl])).astype(BF16), grads)


def upd2_first(j, rows, flags, s, m, w2t, *refs):
    *grads, send, raw, moment = refs
    half = rows // 2
    at = pl.multiple_of(flags[0] * rows + j * half, 8)
    total = s[...].astype(F32) + m[...].astype(F32)
    new = w2t[pl.ds(at, half), :] + total
    moment[...] = total
    raw[...] = new
    emit(flags, send, 0, new.astype(BF16), grads)


def upd2_next(flags, s, m, raw, moment, colscale, *refs):
    *grads, send = refs
    total = s[...].astype(F32) + m[...].astype(F32)
    new = raw[...] * colscale[...] + DECAY * moment[...] + total
    emit(flags, send, 0, new.astype(BF16), grads)


def column_scale(pieces, t2):
    sq = None
    count = 0
    for p in pieces:
        v = p[...].astype(F32)
        q = jnp.sum(v * v, axis=0, keepdims=True)
        sq = q if sq is None else sq + q
        count += p.shape[0]
    return t2[...] / jnp.sqrt(sq / count + EPS)


def scale_body(n_own, flags, *refs):
    pieces, t2, colscale, outs = refs[:-4], refs[-4], refs[-3], refs[-2:]
    sc = column_scale(pieces, t2)
    colscale[...] = sc
    for side in range(2):
        off = 0
        for p in pieces[side * n_own : (side + 1) * n_own]:
            n = p.shape[0]
            outs[side][off : off + n] = (p[...].astype(F32) * sc).astype(BF16)
            off += n


def hidden_body(block, flags, queries, *refs):
    pieces, hidden, gate_rows, up_rows = refs[:-3], refs[-3], refs[-2], refs[-1]
    part = pieces[0].shape[0] // 2
    for i, p in enumerate(pieces):
        gate_rows[i * part : (i + 1) * part] = p[:part]
        up_rows[i * part : (i + 1) * part] = p[part:]
    q = queries[block]
    gate = dot_nt(q, gate_rows[...])
    up = dot_nt(q, up_rows[...])
    _, act = silu_parts(gate)
    hidden[...] = (act * up).astype(BF16)


def out_body(scaled, n_piece, flags, hidden, *refs):
    pieces, rest = refs[:n_piece], list(refs[n_piece:])
    t2 = rest.pop(0) if scaled else None
    out, stack = rest
    off = 0
    for p in pieces:
        n = p.shape[0]
        stack[off : off + n] = p[...]
        off += n
    n = out.shape[0]
    lhs = hidden[pl.ds(pl.multiple_of(flags[0] * n, 8), n), :]
    res = dot_nn(lhs, stack[...])
    if scaled:
        res = res * column_scale(pieces, t2)
    out[...] = res.astype(BF16)


def lay_body(flags, own0, came0, own1, out, sems):
    width = own0.shape[1]
    mine = pl.ds(pl.multiple_of(flags[2] * width, 128), width)
    other = pl.ds(pl.multiple_of((1 - flags[2]) * width, 128), width)
    for c in copies(
        sems,
        (own0, out.at[0, :, mine]),
        (came0, out.at[0, :, other]),
        (own1, out.at[1, :, mine]),
    ):
        c.wait()


def fin_body(flags, came1, laid, out, sems):
    width = came1.shape[1]
    other = pl.ds(pl.multiple_of((1 - flags[2]) * width, 128), width)
    for c in copies(sems, (came1, out.at[1, :, other])):
        c.wait()


def merged(pieces):
    return pieces[0] if len(pieces) == 1 else jnp.concatenate(pieces, axis=0)


PLAN = (
    (0, None), (1, None), (2, None), (3, 0), (4, 1), (5, 2), (None, 3), (6, 4),
    (7, 5), (8, None), (9, 6), (10, 7), (11, 8), (None, 9), (None, 10), (None, 11),
)


def local(queries, key_tokens, values, learn_rates, w_first, w_second, w_third):
    tok = lax.axis_size("tok")
    heads = lax.axis_size("head")
    tok_i = lax.axis_index("tok")
    head_i = lax.axis_index("head")
    cores = 2
    chips = tok // cores
    tokens, width = key_tokens.shape[1], key_tokens.shape[2]
    inner = w_first.shape[1]
    rows = inner // cores
    part = rows // PARTS
    half = rows // 2
    chunk = (half, width)
    grad_scale = 1.0 / math.sqrt(tokens * tok)
    lined = chips == 4
    chip_i = tok_i // cores
    outer = (chip_i == 0) | (chip_i == chips - 1) if lined else chip_i < 0
    flags = jnp.stack([tok_i % cores, outer.astype(jnp.int32), head_i]).astype(jnp.int32)

    def shift(x, pairs):
        return lax.ppermute(x, "tok", pairs)

    def chip_pairs(to):
        return [(c * cores + i, to[c] * cores + i) for c in range(chips) for i in range(cores)]

    core_pairs = [(i, i ^ 1) for i in range(tok)]
    swap_ends = chip_pairs([1, 0, 3, 2]) if lined else None
    swap_mid = (
        [
            (i, j)
            for i, j in chip_pairs([0, 2, 1, 3])
            if i != j
        ]
        + [(i, j) for i, j in core_pairs if i // cores in (0, chips - 1)]
        if lined
        else None
    )

    full = (inner, width)
    mm = 2 * rows * width * tokens
    gu_shape = ((2 * rows, tokens), F32)
    r_oth = shift(learn_rates, core_pairs)

    def loaded(b):
        k, v = call(
            functools.partial(load_body, b),
            flags,
            (key_tokens, values),
            [((tokens, width), BF16)] * 2,
            hbm=(0, 1),
            sems=2,
        )
        return (k, shift(k, core_pairs), v, shift(v, core_pairs), learn_rates, r_oth)

    held = [loaded(b) for b in range(2)]
    k_own, k_oth, v_own, v_oth = held[0][:4]
    u13, w13, gu_own, partial = call(
        functools.partial(first_body, False, grad_scale, rows),
        flags,
        (k_own, v_own, learn_rates, w_first, w_third),
        [(full, BF16), (full, F32), gu_shape, ((rows, width), F32)],
        3 * mm,
        hbm=(3, 4),
        sems=2,
    )
    gu_oth, g0, g1 = call(
        functools.partial(first_body, True, grad_scale, rows),
        flags,
        (k_oth, v_oth, r_oth, u13, partial),
        [gu_shape, (chunk, BF16), (chunk, BF16)],
        3 * mm,
    )
    w2t, u2t, t2 = call(
        functools.partial(flip_body, rows),
        flags,
        (w_second,),
        [(full, F32), ((rows, width), BF16), ((1, width), F32)],
    )
    g_rest = call(
        functools.partial(second_body, grad_scale, rows),
        flags,
        (gu_own, gu_oth, u2t, *held[0]),
        [(chunk, BF16)] * PARTS,
        6 * mm,
    )
    chunks = 2 * (PARTS + 2)
    grads = {0: [g0], 1: [g1]}
    for j in range(PARTS):
        grads[2 + j] = [g_rest[j]]
    finals, others, state = {}, {}, {}
    first13, next13, next2 = 2, PARTS + 2, 2 * PARTS + 2

    def update(k, s, m, sums):
        b16, f32 = (chunk, BF16), (chunk, F32)
        if k < first13:
            u, raw, mom = call(
                functools.partial(upd2_first, k, rows), flags, (s, m, w2t, *sums), [b16, f32, f32]
            )
            state["w2", k] = (raw, mom)
        elif k < next13:
            j = k - first13
            u, new, mom = call(
                functools.partial(upd13_first, j, rows), flags, (s, m, w13, *sums), [b16, f32, f32]
            )
            state["w13", j] = (new, mom)
        elif k < next2:
            j = k - next13
            (u,) = call(
                functools.partial(upd13_next, j, rows),
                flags,
                (s, m, w13, *state["w13", j], *sums),
                [b16],
            )
        else:
            (u,) = call(
                upd2_next, flags, (s, m, *state["w2", k - next2], state["scale"], *sums), [b16]
            )
        return u

    def arrived(k):
        others[k] = shift(finals[k], core_pairs)
        if k == 1:
            state["scale"], state["u2_own"], state["u2_oth"] = call(
                functools.partial(scale_body, 2),
                flags,
                (finals[0], finals[1], others[0], others[1], t2),
                [((1, width), F32), ((rows, width), BF16), ((rows, width), BF16)],
            )
        if first13 <= k < next13:
            j = k - first13
            g13, g2 = call(
                functools.partial(grad_body, j, grad_scale, 1),
                flags,
                (finals[k], state["u2_own"], *held[1]),
                [(chunk, BF16), ((part, width), BF16)],
                12 * mm // PARTS,
            )
            grads[next13 + j] = [g13]
            grads.setdefault(next2 + j // 2, []).append(g2)

    def produce(b, first, second, t2_in):
        pieces = [finals[k] for k in first] + [others[k] for k in first]
        hidden, *_ = call(
            functools.partial(hidden_body, b),
            flags,
            (queries, *pieces),
            [((tokens, inner), BF16), (full, BF16), (full, BF16)],
            8 * mm,
        )
        scaled = t2_in is not None
        extra = (t2_in,) if scaled else ()

        def rows_of(which, n):
            res, _ = call(
                functools.partial(out_body, scaled, len(second)),
                which,
                (hidden, *second, *extra),
                [((n, width), BF16), (full, BF16)],
                4 * mm * n // tokens,
            )
            return res

        if heads != 2:
            whole = rows_of(jnp.zeros((1,), jnp.int32), tokens)
            return lax.all_to_all(whole, "head", split_axis=0, concat_axis=1, tiled=True)
        n = tokens // 2
        away = rows_of((1 - flags[2:]), n)
        came = lax.ppermute(away, "head", [(0, 1), (1, 0)])
        return rows_of(flags[2:], n), came

    def block0():
        return produce(
            0, range(first13, next13), (state["u2_own"], state["u2_oth"]), None
        )

    def block1():
        second = [finals[next2], finals[next2 + 1], others[next2], others[next2 + 1]]
        return produce(1, range(next13, next2), second, t2)

    if lined:
        flight, sends = {}, {}
        for slot, (inw, out) in enumerate(PLAN):
            if out is None:
                sends[slot] = merged(grads[inw])
            else:
                sums = grads[inw] if inw is not None else []
                sends[slot] = update(out, *flight[out], sums)
            rcv = shift(sends[slot], swap_ends)
            if inw is not None:
                g = merged(grads[inw])
                total = (rcv.astype(F32) + g.astype(F32)).astype(BF16)
            if out is not None:
                finals[out] = jnp.where(outer, rcv, sends[slot])
            if inw is not None:
                flight[inw] = (total, shift(total, swap_mid))
            if out is not None:
                arrived(out)
    else:
        groups = [[c * cores + i for c in range(chips)] for i in range(cores)]
        zero = jnp.zeros(chunk, BF16)
        for k in range(chunks):
            s = lax.psum(merged(grads[k]), "tok", axis_index_groups=groups)
            finals[k] = update(k, s, zero, [])
            arrived(k)
    if heads != 2:
        return jnp.stack([block0(), block1()])
    own0, came0 = block0()
    own1, came1 = block1()
    n = tokens // 2
    shape = [((2, n, 2 * width), BF16)]
    (laid,) = call(lay_body, flags, (own0, came0, own1), shape, out_hbm=True, sems=3)
    (out,) = call(
        fin_body, flags, (came1, laid), shape, hbm=(1,), out_hbm=True, sems=1, alias={2: 0}
    )
    return out


def solution(mesh):
    placed = (
        P(None, ("grp", "tok"), "head"),
        P(None, ("grp", "tok"), "head"),
        P(None, ("grp", "tok"), "head"),
        P(None, "head", ("grp", "tok")),
        P("head", None, None),
        P("head", None, None),
        P("head", None, None),
    )
    return jax.shard_map(
        local,
        mesh=mesh,
        in_specs=placed,
        out_specs=P(None, ("grp", "tok", "head"), None),
        check_vma=False,
    )
```

```python
import functools
import math

import jax
import jax.numpy as jnp
from jax import lax
from jax.experimental import pallas as pl
from jax.experimental.pallas import tpu as pltpu
from jax.sharding import PartitionSpec as P


DECAY = 0.9
EPS = 1e-06
F32 = jnp.float32
BF16 = jnp.bfloat16
NT = (((1,), (1,)), ((), ()))
NN = (((1,), (0,)), ((), ()))
PARTS = 4
GRANT = 16 * 2**20
LOAD_GRANT = (52 * 2**20, 40 * 2**20)
FIRST_GRANT = 48 * 2**20
VMEM = pl.BlockSpec(memory_space=pltpu.VMEM)
SMEM = pl.BlockSpec(memory_space=pltpu.SMEM)
HBM = pl.BlockSpec(memory_space=pltpu.HBM)


def dot_nt(a, b):
    return lax.dot_general(a, b, NT, preferred_element_type=F32)


def dot_nn(a, b):
    return lax.dot_general(a, b, NN, preferred_element_type=F32)


def call(
    body, flags, operands, outs, flops=0, hbm=(), out_hbm=False, sems=0, alias=None, grant=GRANT, scalars=False
):
    shapes = [jax.ShapeDtypeStruct(s, d) for s, d in outs]
    moved = sum(math.prod(o.shape) * o.dtype.itemsize for o in list(operands) + shapes)
    return pl.pallas_call(
        body,
        out_shape=shapes,
        in_specs=[SMEM if scalars else VMEM]
        + [HBM if i in hbm else VMEM for i in range(len(operands))],
        out_specs=[HBM if out_hbm else VMEM] * len(shapes),
        scratch_shapes=[pltpu.SemaphoreType.DMA((sems,))] if sems else [],
        input_output_aliases=alias or {},
        compiler_params=pltpu.CompilerParams(vmem_limit_bytes=grant),
        cost_estimate=pl.CostEstimate(
            flops=int(flops), bytes_accessed=int(moved), transcendentals=0
        ),
    )(flags[0] if scalars else flags[1], *operands)


def copies(sems, *pairs):
    started = [pltpu.make_async_copy(src, dst, sems.at[i]) for i, (src, dst) in enumerate(pairs)]
    for c in started:
        c.start()
    return started


def load_body(block, flags, keys, vals, k_out, v_out, sems):
    for c in copies(sems, (keys.at[block], k_out), (vals.at[block], v_out)):
        c.wait()


def silu_parts(gate):
    sig = jax.nn.sigmoid(gate)
    return sig, gate * sig


def row_scale(before, after):
    target = jnp.sqrt(jnp.mean(before * before, axis=-1, keepdims=True) + EPS)
    return target / jnp.sqrt(jnp.mean(after * after, axis=-1, keepdims=True) + EPS)


CORE, OUTER, HEAD = 0, 1, 2


def is_set(flags, which):
    return flags[which : which + 1, :] != 0


def first_body(last, scale, rows, flags, keys, vals, rates, *refs):
    if last:
        u13, partial, g0, g1 = refs
    else:
        w1, w3, u13, w13, partial, sems = refs
        at = pl.multiple_of(flags[CORE] * rows, 8)
        started = copies(
            sems,
            (w1.at[0, pl.ds(at, rows)], w13.at[pl.ds(0, rows)]),
            (w3.at[0, pl.ds(at, rows)], w13.at[pl.ds(rows, rows)]),
        )
        for c in started:
            c.wait()
        u13[...] = w13[...].astype(BF16)
    both = dot_nt(u13[...], keys[...])
    _, act = silu_parts(both[:rows])
    hidden = (act * both[rows:] * rates[0]).astype(BF16)
    grad = dot_nn(hidden, vals[...])
    if last:
        total = ((grad + partial[...]) * scale).astype(BF16)
        g0[...] = total[: rows // 2]
        g1[...] = total[rows // 2 :]
    else:
        partial[...] = grad


def flip_body(rows, flags, w2, w2t, u2t, t2):
    flipped = w2[0].T
    t2[...] = jnp.sqrt(jnp.mean(flipped * flipped, axis=0, keepdims=True) + EPS)
    mine = jnp.where(is_set(flags, CORE), flipped[rows:], flipped[:rows])
    w2t[...] = mine
    u2t[...] = mine.astype(BF16)


def slopes(both, back, part):
    gate, up = both[:part], both[part:]
    sig, act = silu_parts(gate)
    stack = jnp.concatenate(
        [back * up * sig * (1.0 + gate * (1.0 - sig)), back * act], axis=0
    ).astype(BF16)
    return stack, act * up


def second_body(scale, rows, flags, u13, u2t, k_own, k_oth, v_own, v_oth, r_own, r_oth, *outs):
    grad = None
    for keys, vals, rates in ((k_own, v_own, r_own), (k_oth, v_oth, r_oth)):
        back = dot_nt(u2t[...], vals[...]) * rates[0]
        stack, _ = slopes(dot_nt(u13[...], keys[...]), back, rows)
        one = dot_nn(stack, keys[...])
        grad = one if grad is None else grad + one
    grad = (grad * scale).astype(BF16)
    part = rows // PARTS
    for j, out in enumerate(outs):
        out[:part] = grad[j * part : (j + 1) * part]
        out[part:] = grad[rows + j * part : rows + (j + 1) * part]


def grad_body(j, scale, block, flags, new13, u2t, k_own, k_oth, v_own, v_oth, r_own, r_oth, g13, g2):
    part = new13.shape[0] // 2
    w13 = new13[...]
    w2 = u2t[j * part : (j + 1) * part]
    sum13 = sum2 = None
    for keys, vals, rates in ((k_own, v_own, r_own), (k_oth, v_oth, r_oth)):
        kept, rhs = keys[...], vals[...]
        both = dot_nt(w13, kept)
        back = dot_nt(w2, rhs) * rates[block]
        stack, hidden = slopes(both, back, part)
        a = dot_nn(stack, kept)
        b = dot_nn((hidden * rates[block]).astype(BF16), rhs)
        sum13 = a if sum13 is None else sum13 + a
        sum2 = b if sum2 is None else sum2 + b
    g13[...] = (sum13 * scale).astype(BF16)
    g2[...] = (sum2 * scale).astype(BF16)


def emit(flags, out, at, new, grads):
    n = new.shape[0]
    off = 0
    for g in grads:
        lo, hi = max(at, off), min(at + n, off + g.shape[0])
        if lo < hi:
            out[lo:hi] = jnp.where(
                is_set(flags, OUTER), g[lo - off : hi - off].astype(F32), new[lo - at : hi - at]
            ).astype(BF16)
        off += g.shape[0]
    if not grads:
        out[at : at + n] = new.astype(BF16)


def upd13_first(j, rows, flags, s, m, w13, *refs):
    *grads, send, w_new, moment = refs
    part = rows // PARTS
    total = s[...].astype(F32) + m[...].astype(F32)
    moment[...] = total
    for i in range(2):
        sl = slice(i * part, (i + 1) * part)
        old = w13[i * rows + j * part : i * rows + (j + 1) * part]
        new = old + total[sl]
        new = new * row_scale(old, new)
        w_new[sl] = new
        emit(flags, send, i * part, new, grads)


def upd13_next(j, rows, flags, s, m, w13, w_old, moment, *refs):
    *grads, send = refs
    part = rows // PARTS
    new = w_old[...] + DECAY * moment[...] + (s[...].astype(F32) + m[...].astype(F32))
    for i in range(2):
        sl = slice(i * part, (i + 1) * part)
        old = w13[i * rows + j * part : i * rows + (j + 1) * part]
        emit(flags, send, i * part, new[sl] * row_scale(old, new[sl]), grads)


def upd2_first(j, rows, flags, s, m, w2t, *refs):
    *grads, send, raw, moment = refs
    half = rows // 2
    total = s[...].astype(F32) + m[...].astype(F32)
    new = w2t[j * half : (j + 1) * half] + total
    moment[...] = total
    raw[...] = new
    emit(flags, send, 0, new, grads)


def upd2_next(flags, s, m, raw, moment, colscale, *refs):
    *grads, send = refs
    total = s[...].astype(F32) + m[...].astype(F32)
    new = raw[...] * colscale[...] + DECAY * moment[...] + total
    emit(flags, send, 0, new, grads)


def column_scale(pieces, t2):
    sq = None
    count = 0
    for p in pieces:
        v = p[...].astype(F32)
        q = jnp.sum(v * v, axis=0, keepdims=True)
        sq = q if sq is None else sq + q
        count += p.shape[0]
    return t2[...] / jnp.sqrt(sq / count + EPS)


def scale_body(n_own, flags, *refs):
    pieces, t2, colscale, outs = refs[:-4], refs[-4], refs[-3], refs[-2:]
    sc = column_scale(pieces, t2)
    colscale[...] = sc
    for side in range(2):
        off = 0
        for p in pieces[side * n_own : (side + 1) * n_own]:
            n = p.shape[0]
            outs[side][off : off + n] = (p[...].astype(F32) * sc).astype(BF16)
            off += n


def hidden_body(block, flags, queries, *refs):
    pieces, hidden, gate_rows, up_rows = refs[:-3], refs[-3], refs[-2], refs[-1]
    part = pieces[0].shape[0] // 2
    for i, p in enumerate(pieces):
        gate_rows[i * part : (i + 1) * part] = p[:part]
        up_rows[i * part : (i + 1) * part] = p[part:]
    q = queries[block]
    gate = dot_nt(q, gate_rows[...])
    up = dot_nt(q, up_rows[...])
    _, act = silu_parts(gate)
    hidden[...] = (act * up).astype(BF16)


def out_body(scaled, n_piece, picks, flags, hidden, *refs):
    pieces, rest = refs[:n_piece], list(refs[n_piece:])
    t2 = rest.pop(0) if scaled else None
    *outs, stack = rest
    off = 0
    for p in pieces:
        n = p.shape[0]
        stack[off : off + n] = p[...]
        off += n
    rhs = stack[...]
    for pick, out in zip(picks, outs):
        n = out.shape[0]
        lhs = hidden[:n]
        if pick is not None:
            first, second = (lhs, hidden[n:]) if pick == 0 else (hidden[n:], lhs)
            lhs = jnp.where(is_set(flags, HEAD), second.astype(F32), first.astype(F32)).astype(BF16)
        res = dot_nn(lhs, rhs)
        if scaled:
            res = res * column_scale(pieces, t2)
        out[...] = res.astype(BF16)


def lay_body(flags, own0, came0, own1, out, sems):
    width = own0.shape[1]
    mine = pl.ds(pl.multiple_of(flags[HEAD] * width, 128), width)
    other = pl.ds(pl.multiple_of((1 - flags[HEAD]) * width, 128), width)
    for c in copies(
        sems,
        (own0, out.at[0, :, mine]),
        (came0, out.at[0, :, other]),
        (own1, out.at[1, :, mine]),
    ):
        c.wait()


def fin_body(flags, came1, laid, out, sems):
    width = came1.shape[1]
    other = pl.ds(pl.multiple_of((1 - flags[HEAD]) * width, 128), width)
    for c in copies(sems, (came1, out.at[1, :, other])):
        c.wait()


def merged(pieces):
    return pieces[0] if len(pieces) == 1 else jnp.concatenate(pieces, axis=0)


PLAN = (
    (0, None), (1, None), (2, None), (3, 0), (4, 1), (5, 2), (None, 3), (6, 4),
    (7, 5), (8, None), (9, 6), (10, 7), (11, 8), (None, 9), (None, 10), (None, 11),
)


def local(queries, key_tokens, values, learn_rates, w_first, w_second, w_third):
    tok = lax.axis_size("tok")
    heads = lax.axis_size("head")
    cores = 2
    chips = tok // cores
    tokens, width = key_tokens.shape[1], key_tokens.shape[2]
    inner = w_first.shape[1]
    rows = inner // cores
    part = rows // PARTS
    half = rows // 2
    chunk = (half, width)
    grad_scale = 1.0 / math.sqrt(tokens * tok)
    lined = chips == 4
    tok_i = lax.axis_index("tok")
    chip_i = lax.div(tok_i, cores)
    outer = (chip_i == 0) | (chip_i == chips - 1) if lined else chip_i < 0
    place = jnp.stack(
        [lax.rem(tok_i, cores), outer.astype(jnp.int32), lax.axis_index("head")]
    ).astype(jnp.int32)
    flags = (place, jnp.broadcast_to(place[:, None], (3, width)))

    def shift(x, pairs):
        return lax.ppermute(x, "tok", pairs)

    def chip_pairs(to):
        return [(c * cores + i, to[c] * cores + i) for c in range(chips) for i in range(cores)]

    core_pairs = [(i, i ^ 1) for i in range(tok)]
    swap_ends = chip_pairs([1, 0, 3, 2]) if lined else None
    swap_mid = (
        [
            (i, j)
            for i, j in chip_pairs([0, 2, 1, 3])
            if i != j
        ]
        + [(i, j) for i, j in core_pairs if i // cores in (0, chips - 1)]
        if lined
        else None
    )

    full = (inner, width)
    mm = 2 * rows * width * tokens
    r_oth = shift(learn_rates, core_pairs)

    def loaded(b):
        k, v = call(
            functools.partial(load_body, b),
            flags,
            (key_tokens, values),
            [((tokens, width), BF16)] * 2,
            hbm=(0, 1),
            sems=2,
            grant=LOAD_GRANT[b],
        )
        return (k, shift(k, core_pairs), v, shift(v, core_pairs), learn_rates, r_oth)

    held = [loaded(b) for b in range(2)]
    k_own, k_oth, v_own, v_oth = held[0][:4]
    u13, w13, partial = call(
        functools.partial(first_body, False, grad_scale, rows),
        flags,
        (k_own, v_own, learn_rates, w_first, w_third),
        [(full, BF16), (full, F32), ((rows, width), F32)],
        3 * mm,
        hbm=(3, 4),
        sems=2,
        grant=FIRST_GRANT,
        scalars=True,
    )
    g0, g1 = call(
        functools.partial(first_body, True, grad_scale, rows),
        flags,
        (k_oth, v_oth, r_oth, u13, partial),
        [(chunk, BF16), (chunk, BF16)],
        3 * mm,
    )
    w2t, u2t, t2 = call(
        functools.partial(flip_body, rows),
        flags,
        (w_second,),
        [((rows, width), F32), ((rows, width), BF16), ((1, width), F32)],
    )
    g_rest = call(
        functools.partial(second_body, grad_scale, rows),
        flags,
        (u13, u2t, *held[0]),
        [(chunk, BF16)] * PARTS,
        10 * mm,
    )
    chunks = 2 * (PARTS + 2)
    grads = {0: [g0], 1: [g1]}
    for j in range(PARTS):
        grads[2 + j] = [g_rest[j]]
    finals, others, state = {}, {}, {}
    first13, next13, next2 = 2, PARTS + 2, 2 * PARTS + 2

    def gradient(j):
        g13, g2 = call(
            functools.partial(grad_body, j, grad_scale, 1),
            flags,
            (finals[first13 + j], state["u2_own"], *held[1]),
            [(chunk, BF16), ((part, width), BF16)],
            12 * mm // PARTS,
        )
        grads[next13 + j] = [g13]
        grads.setdefault(next2 + j // 2, []).append(g2)

    def update(k, s, m, inw):
        b16, f32 = (chunk, BF16), (chunk, F32)
        if k < first13:
            body, ins, outs = functools.partial(upd2_first, k, rows), (w2t,), [b16, f32, f32]
        elif k < next13:
            body = functools.partial(upd13_first, k - first13, rows)
            ins, outs = (w13,), [b16, f32, f32]
        elif k < next2:
            body = functools.partial(upd13_next, k - next13, rows)
            ins, outs = (w13, *state[first13 + k - next13]), [b16]
        else:
            body, ins, outs = upd2_next, (*state[k - next2], state["scale"]), [b16]
        sums = grads[inw] if inw is not None else []
        u, *state[k] = call(body, flags, (s, m, *ins, *sums), outs)
        return u

    def arrived(k):
        others[k] = shift(finals[k], core_pairs)
        if k == 1:
            state["scale"], state["u2_own"], state["u2_oth"] = call(
                functools.partial(scale_body, 2),
                flags,
                (finals[0], finals[1], others[0], others[1], t2),
                [((1, width), F32), ((rows, width), BF16), ((rows, width), BF16)],
            )

    def produce(b, first, second, t2_in):
        pieces = [finals[k] for k in first] + [others[k] for k in first]
        hidden, *_ = call(
            functools.partial(hidden_body, b),
            flags,
            (queries, *pieces),
            [((tokens, inner), BF16), (full, BF16), (full, BF16)],
            8 * mm,
        )
        scaled = t2_in is not None
        extra = (t2_in,) if scaled else ()

        def rows_of(picks, n):
            *res, _ = call(
                functools.partial(out_body, scaled, len(second), picks),
                flags,
                (hidden, *second, *extra),
                [((n, width), BF16)] * len(picks) + [(full, BF16)],
                4 * mm * n * len(picks) // tokens,
            )
            return res

        if heads != 2:
            (whole,) = rows_of((None,), tokens)
            return lax.all_to_all(whole, "head", split_axis=0, concat_axis=1, tiled=True)
        n = tokens // 2
        if b == 0:
            away, own = rows_of((1, 0), n)
        else:
            (away,) = rows_of((1,), n)
            (own,) = rows_of((0,), n)
        came = lax.ppermute(away, "head", [(0, 1), (1, 0)])
        return own, came

    def block0():
        return produce(
            0, range(first13, next13), (state["u2_own"], state["u2_oth"]), None
        )

    def block1():
        second = [finals[next2], finals[next2 + 1], others[next2], others[next2 + 1]]
        return produce(1, range(next13, next2), second, t2)

    if lined:
        flight, sends = {}, {}
        for slot, (inw, out) in enumerate(PLAN):
            if inw is not None and inw not in grads:
                gradient(inw - next13)
            if out is not None:
                sends[slot] = update(out, *flight[out], inw)
            else:
                sends[slot] = merged(grads[inw])
            rcv = shift(sends[slot], swap_ends)
            if inw is not None:
                g = merged(grads[inw])
                total = (rcv.astype(F32) + g.astype(F32)).astype(BF16)
            if out is not None:
                finals[out] = jnp.where(outer, rcv, sends[slot])
            if inw is not None:
                flight[inw] = (total, shift(total, swap_mid))
            if out is not None:
                arrived(out)
    else:
        groups = [[c * cores + i for c in range(chips)] for i in range(cores)]
        zero = jnp.zeros(chunk, BF16)
        for k in range(chunks):
            if k not in grads:
                gradient(k - next13)
            s = lax.psum(merged(grads[k]), "tok", axis_index_groups=groups)
            finals[k] = update(k, s, zero, None)
            arrived(k)
    if heads != 2:
        return jnp.stack([block0(), block1()])
    own0, came0 = block0()
    own1, came1 = block1()
    n = tokens // 2
    shape = [((2, n, 2 * width), BF16)]
    (laid,) = call(lay_body, flags, (own0, came0, own1), shape, out_hbm=True, sems=3, scalars=True)
    (out,) = call(
        fin_body,
        flags,
        (came1, laid),
        shape,
        hbm=(1,),
        out_hbm=True,
        sems=1,
        alias={2: 0},
        scalars=True,
    )
    return out


def solution(mesh):
    placed = (
        P(None, ("grp", "tok"), "head"),
        P(None, ("grp", "tok"), "head"),
        P(None, ("grp", "tok"), "head"),
        P(None, "head", ("grp", "tok")),
        P("head", None, None),
        P("head", None, None),
        P("head", None, None),
    )
    return jax.shard_map(
        local,
        mesh=mesh,
        in_specs=placed,
        out_specs=P(None, ("grp", "tok", "head"), None),
        check_vma=False,
    )
```

```python
import functools
import math

import jax
import jax.numpy as jnp
from jax import lax
from jax.experimental import pallas as pl
from jax.experimental.pallas import tpu as pltpu
from jax.sharding import PartitionSpec as P


DECAY = 0.9
EPS = 1e-06
F32 = jnp.float32
BF16 = jnp.bfloat16
NT = (((1,), (1,)), ((), ()))
NN = (((1,), (0,)), ((), ()))
PARTS = 4
GRANT = 16 * 2**20
LOAD_GRANT = (52 * 2**20, 40 * 2**20)
FIRST_GRANT = 48 * 2**20
VMEM = pl.BlockSpec(memory_space=pltpu.VMEM)
SMEM = pl.BlockSpec(memory_space=pltpu.SMEM)
HBM = pl.BlockSpec(memory_space=pltpu.HBM)


def dot_nt(a, b):
    return lax.dot_general(a, b, NT, preferred_element_type=F32)


def dot_nn(a, b):
    return lax.dot_general(a, b, NN, preferred_element_type=F32)


def call(
    body, flags, operands, outs, flops=0, hbm=(), out_hbm=False, sems=0, alias=None, grant=GRANT, scalars=False, scratch=()
):
    shapes = [jax.ShapeDtypeStruct(s, d) for s, d in outs]
    moved = sum(math.prod(o.shape) * o.dtype.itemsize for o in list(operands) + shapes)
    return pl.pallas_call(
        body,
        out_shape=shapes,
        in_specs=[SMEM if scalars else VMEM]
        + [HBM if i in hbm else VMEM for i in range(len(operands))],
        out_specs=[HBM if out_hbm else VMEM] * len(shapes),
        scratch_shapes=[pltpu.VMEM(*x) for x in scratch]
        + ([pltpu.SemaphoreType.DMA((sems,))] if sems else []),
        input_output_aliases=alias or {},
        compiler_params=pltpu.CompilerParams(vmem_limit_bytes=grant),
        cost_estimate=pl.CostEstimate(
            flops=int(flops), bytes_accessed=int(moved), transcendentals=0
        ),
    )(flags[0] if scalars else flags[1], *operands)


def copies(sems, *pairs):
    started = [pltpu.make_async_copy(src, dst, sems.at[i]) for i, (src, dst) in enumerate(pairs)]
    for c in started:
        c.start()
    return started


def load_body(block, flags, keys, vals, k_out, v_out, sems):
    for c in copies(sems, (keys.at[block], k_out), (vals.at[block], v_out)):
        c.wait()


def silu_parts(gate):
    sig = jax.nn.sigmoid(gate)
    return sig, gate * sig


def row_scale(before, after):
    target = jnp.sqrt(jnp.mean(before * before, axis=-1, keepdims=True) + EPS)
    return target / jnp.sqrt(jnp.mean(after * after, axis=-1, keepdims=True) + EPS)


CORE, OUTER, HEAD = 0, 1, 2


def is_set(flags, which):
    return flags[which : which + 1, :] != 0


def first_body(last, scale, rows, flags, keys, vals, rates, *refs):
    if last:
        u13, partial, g0, g1 = refs
    else:
        w1, w3, u13, w13, partial, sems = refs
        at = pl.multiple_of(flags[CORE] * rows, 8)
        started = copies(
            sems,
            (w1.at[0, pl.ds(at, rows)], w13.at[pl.ds(0, rows)]),
            (w3.at[0, pl.ds(at, rows)], w13.at[pl.ds(rows, rows)]),
        )
        for c in started:
            c.wait()
        u13[...] = w13[...].astype(BF16)
    both = dot_nt(u13[...], keys[...])
    _, act = silu_parts(both[:rows])
    hidden = (act * both[rows:] * rates[0]).astype(BF16)
    grad = dot_nn(hidden, vals[...])
    if last:
        total = ((grad + partial[...]) * scale).astype(BF16)
        g0[...] = total[: rows // 2]
        g1[...] = total[rows // 2 :]
    else:
        partial[...] = grad


def flip_body(rows, flags, w2, w2t, u2t, t2):
    flipped = w2[0].T
    t2[...] = jnp.sqrt(jnp.mean(flipped * flipped, axis=0, keepdims=True) + EPS)
    mine = jnp.where(is_set(flags, CORE), flipped[rows:], flipped[:rows])
    w2t[...] = mine
    u2t[...] = mine.astype(BF16)


def slopes(both, back, part):
    gate, up = both[:part], both[part:]
    sig, act = silu_parts(gate)
    stack = jnp.concatenate(
        [back * up * sig * (1.0 + gate * (1.0 - sig)), back * act], axis=0
    ).astype(BF16)
    return stack, act * up


def second_body(scale, rows, flags, u13, u2t, k_own, k_oth, v_own, v_oth, r_own, r_oth, *outs):
    grad = None
    for keys, vals, rates in ((k_own, v_own, r_own), (k_oth, v_oth, r_oth)):
        back = dot_nt(u2t[...], vals[...]) * rates[0]
        stack, _ = slopes(dot_nt(u13[...], keys[...]), back, rows)
        one = dot_nn(stack, keys[...])
        grad = one if grad is None else grad + one
    grad = (grad * scale).astype(BF16)
    part = rows // PARTS
    for j, out in enumerate(outs):
        out[:part] = grad[j * part : (j + 1) * part]
        out[part:] = grad[rows + j * part : rows + (j + 1) * part]


def grad_body(j, scale, block, flags, new13, u2t, k_own, k_oth, v_own, v_oth, r_own, r_oth, g13, g2):
    part = new13.shape[0] // 2
    w13 = new13[...]
    w2 = u2t[j * part : (j + 1) * part]
    sum13 = sum2 = None
    for keys, vals, rates in ((k_own, v_own, r_own), (k_oth, v_oth, r_oth)):
        kept, rhs = keys[...], vals[...]
        both = dot_nt(w13, kept)
        back = dot_nt(w2, rhs) * rates[block]
        stack, hidden = slopes(both, back, part)
        a = dot_nn(stack, kept)
        b = dot_nn((hidden * rates[block]).astype(BF16), rhs)
        sum13 = a if sum13 is None else sum13 + a
        sum2 = b if sum2 is None else sum2 + b
    g13[...] = (sum13 * scale).astype(BF16)
    g2[...] = (sum2 * scale).astype(BF16)


def emit(flags, out, at, new, grads):
    n = new.shape[0]
    off = 0
    for g in grads:
        lo, hi = max(at, off), min(at + n, off + g.shape[0])
        if lo < hi:
            out[lo:hi] = jnp.where(
                is_set(flags, OUTER), g[lo - off : hi - off].astype(F32), new[lo - at : hi - at]
            ).astype(BF16)
        off += g.shape[0]
    if not grads:
        out[at : at + n] = new.astype(BF16)


def both(s, m):
    return s[...].astype(F32) + m[...].astype(F32)


def upd13_body(j, rows, flags, s, m, w13, *refs):
    *more, send = refs
    prior, grads = (more[:2], more[2:]) if len(more) > 1 else ((), more)
    part = rows // PARTS
    total = both(s, m)
    before = both(*prior) if prior else None
    for i in range(2):
        sl = slice(i * part, (i + 1) * part)
        first = old = w13[i * rows + j * part : i * rows + (j + 1) * part]
        moment = total[sl]
        if prior:
            old = first + before[sl]
            old = old * row_scale(first, old)
            moment = DECAY * before[sl] + moment
        new = old + moment
        emit(flags, send, i * part, new * row_scale(first, new), grads)


def upd2_first(j, rows, flags, s, m, w2t, *refs):
    *grads, send = refs
    half = rows // 2
    emit(flags, send, 0, w2t[j * half : (j + 1) * half] + both(s, m), grads)


def split(width):
    return width // 2 // 128 * 128


def packing(j, cut):
    head = slice(j * cut, (j + 1) * cut)
    return ((0, head), (1, head), (j, slice(2 * cut, None)))


def pack_body(cut, flags, *refs):
    pieces, outs = refs[:PARTS], refs[PARTS:]
    side = PARTS // 2
    for j, out in enumerate(outs):
        lane = 0
        for half, cols in packing(j, cut):
            row = 0
            for p in pieces[half * side : (half + 1) * side]:
                part = p[:, cols]
                out[row : row + part.shape[0], lane : lane + part.shape[1]] = part
                row += part.shape[0]
            lane += part.shape[1]


def upd2_next(j, cut, flags, s, m, w2t, s0, m0, s1, m1, colscale, *refs):
    *grads, send = refs
    half = s.shape[0]
    gain = colscale[...]
    moved = []
    for part, cols in packing(j, cut):
        sums, met = ((s0, m0), (s1, m1))[part]
        before = sums[:, cols].astype(F32) + met[:, cols].astype(F32)
        old = (w2t[part * half : (part + 1) * half, cols] + before) * gain[:, cols]
        moved.append(old + DECAY * before)
    emit(flags, send, 0, jnp.concatenate(moved, axis=1) + both(s, m), grads)


def column_scale(pieces, t2):
    sq = None
    count = 0
    for p in pieces:
        v = p[...].astype(F32)
        q = jnp.sum(v * v, axis=0, keepdims=True)
        sq = q if sq is None else sq + q
        count += p.shape[0]
    return t2 / jnp.sqrt(sq / count + EPS)


def scale_body(n_own, flags, *refs):
    pieces, t2, colscale, outs = refs[:-4], refs[-4], refs[-3], refs[-2:]
    sc = column_scale(pieces, t2[...])
    colscale[...] = sc
    for side in range(2):
        off = 0
        for p in pieces[side * n_own : (side + 1) * n_own]:
            n = p.shape[0]
            outs[side][off : off + n] = (p[...].astype(F32) * sc).astype(BF16)
            off += n


def hidden_body(block, flags, queries, *refs):
    *pieces, hidden, gate_rows, up_rows = refs
    part = pieces[0].shape[0] // 2
    for i, p in enumerate(pieces):
        gate_rows[i * part : (i + 1) * part] = p[:part]
        up_rows[i * part : (i + 1) * part] = p[part:]
    q = queries[block]
    gate = dot_nt(q, gate_rows[...])
    up = dot_nt(q, up_rows[...])
    _, act = silu_parts(gate)
    hidden[...] = (act * up).astype(BF16)


def pick_rows(flags, hidden, pick, n):
    if pick is None:
        return hidden[...]
    low, high = hidden[:n], hidden[n:]
    first, second = (low, high) if pick == 0 else (high, low)
    return jnp.where(is_set(flags, HEAD), second.astype(F32), first.astype(F32)).astype(BF16)


def out0_body(picks, flags, hidden, u2_own, u2_oth, *refs):
    *outs, stack = refs
    n = u2_own.shape[0]
    stack[:n] = u2_own[...]
    stack[n:] = u2_oth[...]
    for pick, out in zip(picks, outs):
        lhs = pick_rows(flags, hidden, pick, out.shape[0])
        out[...] = dot_nn(lhs, stack[...]).astype(BF16)


def out1_body(picks, which, cut, flags, hidden, a_own, a_oth, *refs):
    refs = list(refs)
    b_own, b_oth = (refs.pop(0), refs.pop(0)) if which else (None, None)
    t2, *outs, stack = refs
    half = a_own.shape[0]
    row = 0
    for a, b in ((a_own, b_own), (a_oth, b_oth)):
        for part in range(2):
            at = slice(row, row + half)
            src = b if which else a
            stack[at, :cut] = src[:, part * cut : (part + 1) * cut]
            if which:
                stack[at, cut:] = (a, b)[part][:, 2 * cut :]
            row += half
    rhs = stack[...]
    for pick, out in zip(picks, outs):
        res = dot_nn(pick_rows(flags, hidden, pick, out.shape[0]), rhs)
        cols = slice(cut, None) if which else slice(0, cut)
        out[...] = (res * column_scale((stack,), t2[:, cols])).astype(BF16)


def columns(flags, width, mine):
    head = flags[HEAD] if mine else 1 - flags[HEAD]
    return pl.multiple_of(head * width, 128)


def lay_body(width, cut, flags, own0, came0, own_a, own_b, came_a, out, sems):
    mine, other = columns(flags, width, True), columns(flags, width, False)
    for c in copies(
        sems,
        (own0, out.at[0, :, pl.ds(mine, width)]),
        (came0, out.at[0, :, pl.ds(other, width)]),
        (own_a, out.at[1, :, pl.ds(mine, cut)]),
        (own_b, out.at[1, :, pl.ds(mine + cut, width - cut)]),
        (came_a, out.at[1, :, pl.ds(other, cut)]),
    ):
        c.wait()


def fin_body(width, cut, flags, came_b, laid, out, sems):
    other = columns(flags, width, False)
    for c in copies(sems, (came_b, out.at[1, :, pl.ds(other + cut, width - cut)])):
        c.wait()


def merged(pieces):
    return pieces[0] if len(pieces) == 1 else jnp.concatenate(pieces, axis=0)


PLAN = (
    (0, None), (1, None), (2, None), (3, 0), (4, 1), (5, 2), (None, 3), (6, 4),
    (7, 5), (8, None), (9, 6), (10, 7), (11, 8), (None, 9), (None, 10), (None, 11),
)


def local(queries, key_tokens, values, learn_rates, w_first, w_second, w_third):
    tok = lax.axis_size("tok")
    heads = lax.axis_size("head")
    cores = 2
    chips = tok // cores
    tokens, width = key_tokens.shape[1], key_tokens.shape[2]
    inner = w_first.shape[1]
    rows = inner // cores
    part = rows // PARTS
    half = rows // 2
    chunk = (half, width)
    grad_scale = 1.0 / math.sqrt(tokens * tok)
    lined = chips == 4
    tok_i = lax.axis_index("tok")
    chip_i = lax.div(tok_i, cores)
    outer = (chip_i == 0) | (chip_i == chips - 1) if lined else chip_i < 0
    place = jnp.stack(
        [lax.rem(tok_i, cores), outer.astype(jnp.int32), lax.axis_index("head")]
    ).astype(jnp.int32)
    flags = (place, jnp.broadcast_to(place[:, None], (3, width)))

    def shift(x, pairs):
        return lax.ppermute(x, "tok", pairs)

    def chip_pairs(to):
        return [(c * cores + i, to[c] * cores + i) for c in range(chips) for i in range(cores)]

    core_pairs = [(i, i ^ 1) for i in range(tok)]
    swap_ends = chip_pairs([1, 0, 3, 2]) if lined else None
    swap_mid = (
        [
            (i, j)
            for i, j in chip_pairs([0, 2, 1, 3])
            if i != j
        ]
        + [(i, j) for i, j in core_pairs if i // cores in (0, chips - 1)]
        if lined
        else None
    )

    full = (inner, width)
    mm = 2 * rows * width * tokens
    r_oth = shift(learn_rates, core_pairs)

    def loaded(b):
        k, v = call(
            functools.partial(load_body, b),
            flags,
            (key_tokens, values),
            [((tokens, width), BF16)] * 2,
            hbm=(0, 1),
            sems=2,
            grant=LOAD_GRANT[b],
        )
        return (k, shift(k, core_pairs), v, shift(v, core_pairs), learn_rates, r_oth)

    held = [loaded(b) for b in range(2)]
    k_own, k_oth, v_own, v_oth = held[0][:4]
    u13, w13, partial = call(
        functools.partial(first_body, False, grad_scale, rows),
        flags,
        (k_own, v_own, learn_rates, w_first, w_third),
        [(full, BF16), (full, F32), ((rows, width), F32)],
        3 * mm,
        hbm=(3, 4),
        sems=2,
        grant=FIRST_GRANT,
        scalars=True,
    )
    g0, g1 = call(
        functools.partial(first_body, True, grad_scale, rows),
        flags,
        (k_oth, v_oth, r_oth, u13, partial),
        [(chunk, BF16), (chunk, BF16)],
        3 * mm,
    )
    w2t, u2t, t2 = call(
        functools.partial(flip_body, rows),
        flags,
        (w_second,),
        [((rows, width), F32), ((rows, width), BF16), ((1, width), F32)],
    )
    g_rest = call(
        functools.partial(second_body, grad_scale, rows),
        flags,
        (u13, u2t, *held[0]),
        [(chunk, BF16)] * PARTS,
        10 * mm,
    )
    chunks = 2 * (PARTS + 2)
    grads = {0: [g0], 1: [g1]}
    for j in range(PARTS):
        grads[2 + j] = [g_rest[j]]
    finals, others, state = {}, {}, {}
    first13, next13, next2 = 2, PARTS + 2, 2 * PARTS + 2

    cut = split(width)
    seconds = []

    def gradient(j):
        g13, g2 = call(
            functools.partial(grad_body, j, grad_scale, 1),
            flags,
            (finals[first13 + j], state["u2_own"], *held[1]),
            [(chunk, BF16), ((part, width), BF16)],
            12 * mm // PARTS,
        )
        grads[next13 + j] = [g13]
        seconds.append(g2)
        if j == PARTS - 1:
            packed = call(
                functools.partial(pack_body, cut), flags, seconds, [(chunk, BF16)] * 2
            )
            for i, g in enumerate(packed):
                grads[next2 + i] = [g]

    def update(k, s, m, inw):
        state[k] = (s, m)
        if k < first13:
            body, ins = functools.partial(upd2_first, k, rows), (w2t,)
        elif k < next13:
            body, ins = functools.partial(upd13_body, k - first13, rows), (w13,)
        elif k < next2:
            body = functools.partial(upd13_body, k - next13, rows)
            ins = (w13, *state[first13 + k - next13])
        else:
            body = functools.partial(upd2_next, k - next2, cut)
            ins = (w2t, *state[0], *state[1], state["scale"])
        sums = grads[inw] if inw is not None else []
        (u,) = call(body, flags, (s, m, *ins, *sums), [(chunk, BF16)])
        return u

    def arrived(k):
        others[k] = shift(finals[k], core_pairs)
        if k == 1:
            state["scale"], state["u2_own"], state["u2_oth"] = call(
                functools.partial(scale_body, 2),
                flags,
                (finals[0], finals[1], others[0], others[1], t2),
                [((1, width), F32), ((rows, width), BF16), ((rows, width), BF16)],
            )

    def hidden_of(b, first):
        pieces = [finals[k] for k in first] + [others[k] for k in first]
        (hidden,) = call(
            functools.partial(hidden_body, b),
            flags,
            (queries, *pieces),
            [((tokens, inner), BF16)],
            8 * mm,
            scratch=[(full, BF16)] * 2,
        )
        return hidden

    def block0(picks, n):
        hidden = hidden_of(0, range(first13, next13))
        return call(
            functools.partial(out0_body, picks),
            flags,
            (hidden, state["u2_own"], state["u2_oth"]),
            [((n, width), BF16)] * len(picks),
            4 * mm,
            scratch=[(full, BF16)],
        )

    def block1(hidden, which, pick, n):
        ins = [hidden, finals[next2], others[next2]]
        if which:
            ins += [finals[next2 + 1], others[next2 + 1]]
        cols = width - cut if which else cut
        (res,) = call(
            functools.partial(out1_body, (pick,), which, cut),
            flags,
            (*ins, t2),
            [((n, cols), BF16)],
            2 * mm,
            scratch=[((inner, cols), BF16)],
        )
        return res

    def across(x):
        return lax.ppermute(x, "head", [(0, 1), (1, 0)])

    if lined:
        flight, sends = {}, {}
        for slot, (inw, out) in enumerate(PLAN):
            if inw is not None and inw not in grads:
                gradient(inw - next13)
            if out is not None:
                sends[slot] = update(out, *flight[out], inw)
            else:
                sends[slot] = merged(grads[inw])
            rcv = shift(sends[slot], swap_ends)
            if inw is not None:
                g = merged(grads[inw])
                total = (rcv.astype(F32) + g.astype(F32)).astype(BF16)
            if out is not None:
                finals[out] = jnp.where(outer, rcv, sends[slot])
            if inw is not None:
                flight[inw] = (total, shift(total, swap_mid))
            if out is not None:
                arrived(out)
    else:
        groups = [[c * cores + i for c in range(chips)] for i in range(cores)]
        zero = jnp.zeros(chunk, BF16)
        for k in range(chunks):
            if k not in grads:
                gradient(k - next13)
            s = lax.psum(merged(grads[k]), "tok", axis_index_groups=groups)
            finals[k] = update(k, s, zero, None)
            arrived(k)
    if heads != 2:
        (whole0,) = block0((None,), tokens)
        hidden = hidden_of(1, range(next13, next2))
        whole1 = jnp.concatenate(
            [block1(hidden, i, None, tokens) for i in range(2)], axis=1
        )
        return jnp.stack(
            [
                lax.all_to_all(x, "head", split_axis=0, concat_axis=1, tiled=True)
                for x in (whole0, whole1)
            ]
        )
    n = tokens // 2
    away, own0 = block0((1, 0), n)
    came0 = across(away)
    hidden = hidden_of(1, range(next13, next2))
    came_a = across(block1(hidden, 0, 1, n))
    came_b = across(block1(hidden, 1, 1, n))
    own_a = block1(hidden, 0, 0, n)
    own_b = block1(hidden, 1, 0, n)
    shape = [((2, n, 2 * width), BF16)]
    (laid,) = call(
        functools.partial(lay_body, width, cut),
        flags,
        (own0, came0, own_a, own_b, came_a),
        shape,
        out_hbm=True,
        sems=5,
        scalars=True,
    )
    (out,) = call(
        functools.partial(fin_body, width, cut),
        flags,
        (came_b, laid),
        shape,
        hbm=(1,),
        out_hbm=True,
        sems=1,
        alias={2: 0},
        scalars=True,
    )
    return out


def solution(mesh):
    placed = (
        P(None, ("grp", "tok"), "head"),
        P(None, ("grp", "tok"), "head"),
        P(None, ("grp", "tok"), "head"),
        P(None, "head", ("grp", "tok")),
        P("head", None, None),
        P("head", None, None),
        P("head", None, None),
    )
    return jax.shard_map(
        local,
        mesh=mesh,
        in_specs=placed,
        out_specs=P(None, ("grp", "tok", "head"), None),
        check_vma=False,
    )
```

```python
import functools
import math

import jax
import jax.numpy as jnp
from jax import lax
from jax.experimental import pallas as pl
from jax.experimental.pallas import tpu as pltpu
from jax.sharding import PartitionSpec as P


DECAY = 0.9
EPS = 1e-06
F32 = jnp.float32
BF16 = jnp.bfloat16
NT = (((1,), (1,)), ((), ()))
NN = (((1,), (0,)), ((), ()))
PARTS = 4
GRANT = 16 * 2**20
LOAD_GRANT = (52 * 2**20, 40 * 2**20)
FIRST_GRANT = 50 * 2**20
VMEM = pl.BlockSpec(memory_space=pltpu.VMEM)
SMEM = pl.BlockSpec(memory_space=pltpu.SMEM)
HBM = pl.BlockSpec(memory_space=pltpu.HBM)


def dot_nt(a, b):
    return lax.dot_general(a, b, NT, preferred_element_type=F32)


def dot_nn(a, b):
    return lax.dot_general(a, b, NN, preferred_element_type=F32)


def call(
    body, flags, operands, outs, flops=0, hbm=(), out_hbm=False, sems=0, alias=None, grant=GRANT, scalars=False, scratch=()
):
    shapes = [jax.ShapeDtypeStruct(s, d) for s, d in outs]
    moved = sum(math.prod(o.shape) * o.dtype.itemsize for o in list(operands) + shapes)
    return pl.pallas_call(
        body,
        out_shape=shapes,
        in_specs=[SMEM if scalars else VMEM]
        + [HBM if i in hbm else VMEM for i in range(len(operands))],
        out_specs=[HBM if out_hbm else VMEM] * len(shapes),
        scratch_shapes=[pltpu.VMEM(*x) for x in scratch]
        + ([pltpu.SemaphoreType.DMA((sems,))] if sems else []),
        input_output_aliases=alias or {},
        compiler_params=pltpu.CompilerParams(vmem_limit_bytes=grant),
        cost_estimate=pl.CostEstimate(
            flops=int(flops), bytes_accessed=int(moved), transcendentals=0
        ),
    )(flags[0] if scalars else flags[1], *operands)


def copies(sems, *pairs):
    started = [pltpu.make_async_copy(src, dst, sems.at[i]) for i, (src, dst) in enumerate(pairs)]
    for c in started:
        c.start()
    return started


def load_body(block, flags, keys, vals, k_out, v_out, sems):
    for c in copies(sems, (keys.at[block], k_out), (vals.at[block], v_out)):
        c.wait()


def silu_parts(gate):
    sig = jax.nn.sigmoid(gate)
    return sig, gate * sig


def row_scale(before, after):
    target = jnp.sqrt(jnp.mean(before * before, axis=-1, keepdims=True) + EPS)
    return target / jnp.sqrt(jnp.mean(after * after, axis=-1, keepdims=True) + EPS)


CORE, OUTER, HEAD = 0, 1, 2


def is_set(flags, which):
    return flags[which : which + 1, :] != 0


def first_body(last, side, scale, rows, flags, keys, vals, rates, *refs):
    half = rows // 2
    if last:
        u13, partial, out = refs
    else:
        w1, w3, u13, w13, partial, sems = refs
        at = pl.multiple_of(flags[CORE] * rows + side * half, 8)
        started = copies(
            sems,
            (w1.at[0, pl.ds(at, half)], w13.at[pl.ds(0, half)]),
            (w3.at[0, pl.ds(at, half)], w13.at[pl.ds(half, half)]),
        )
        for c in started:
            c.wait()
        u13[...] = w13[...].astype(BF16)
    product = dot_nt(u13[...], keys[...])
    _, act = silu_parts(product[:half])
    hidden = (act * product[half:] * rates[0]).astype(BF16)
    grad = dot_nn(hidden, vals[...])
    if last:
        out[...] = ((grad + partial[...]) * scale).astype(BF16)
    else:
        partial[...] = grad


def flip_body(rows, flags, w2, w2t, u2t, t2):
    flipped = w2[0].T
    t2[...] = jnp.sqrt(jnp.mean(flipped * flipped, axis=0, keepdims=True) + EPS)
    mine = jnp.where(is_set(flags, CORE), flipped[rows:], flipped[:rows])
    w2t[...] = mine
    u2t[...] = mine.astype(BF16)


def slopes(both, back, part):
    gate, up = both[:part], both[part:]
    sig, act = silu_parts(gate)
    stack = jnp.concatenate(
        [back * up * sig * (1.0 + gate * (1.0 - sig)), back * act], axis=0
    ).astype(BF16)
    return stack, act * up


def second_body(
    side, scale, flags, u13, u2t, k_own, k_oth, v_own, v_oth, r_own, r_oth, *outs
):
    half = u13.shape[0] // 2
    w2 = u2t[side * half : (side + 1) * half]
    grad = None
    for keys, vals, rates in ((k_own, v_own, r_own), (k_oth, v_oth, r_oth)):
        back = dot_nt(w2, vals[...]) * rates[0]
        stack, _ = slopes(dot_nt(u13[...], keys[...]), back, half)
        one = dot_nn(stack, keys[...])
        grad = one if grad is None else grad + one
    grad = (grad * scale).astype(BF16)
    part = half // len(outs)
    for j, out in enumerate(outs):
        out[:part] = grad[j * part : (j + 1) * part]
        out[part:] = grad[half + j * part : half + (j + 1) * part]


def grad_body(j, scale, block, flags, new13, u2t, k_own, k_oth, v_own, v_oth, r_own, r_oth, g13, g2):
    part = new13.shape[0] // 2
    w13 = new13[...]
    w2 = u2t[j * part : (j + 1) * part]
    sum13 = sum2 = None
    for keys, vals, rates in ((k_own, v_own, r_own), (k_oth, v_oth, r_oth)):
        kept, rhs = keys[...], vals[...]
        both = dot_nt(w13, kept)
        back = dot_nt(w2, rhs) * rates[block]
        stack, hidden = slopes(both, back, part)
        a = dot_nn(stack, kept)
        b = dot_nn((hidden * rates[block]).astype(BF16), rhs)
        sum13 = a if sum13 is None else sum13 + a
        sum2 = b if sum2 is None else sum2 + b
    g13[...] = (sum13 * scale).astype(BF16)
    g2[...] = (sum2 * scale).astype(BF16)


def emit(flags, out, at, new, grads):
    n = new.shape[0]
    off = 0
    for g in grads:
        lo, hi = max(at, off), min(at + n, off + g.shape[0])
        if lo < hi:
            out[lo:hi] = jnp.where(
                is_set(flags, OUTER), g[lo - off : hi - off].astype(F32), new[lo - at : hi - at]
            ).astype(BF16)
        off += g.shape[0]
    if not grads:
        out[at : at + n] = new.astype(BF16)


def both(s, m):
    return s[...].astype(F32) + m[...].astype(F32)


def upd13_body(j, flags, s, m, w13, *refs):
    *more, send = refs
    prior, grads = (more[:2], more[2:]) if len(more) > 1 else ((), more)
    part, half = s.shape[0] // 2, w13.shape[0] // 2
    total = both(s, m)
    before = both(*prior) if prior else None
    for i in range(2):
        sl = slice(i * part, (i + 1) * part)
        first = old = w13[i * half + j * part : i * half + (j + 1) * part]
        moment = total[sl]
        if prior:
            old = first + before[sl]
            old = old * row_scale(first, old)
            moment = DECAY * before[sl] + moment
        new = old + moment
        emit(flags, send, i * part, new * row_scale(first, new), grads)


def upd2_first(j, rows, flags, s, m, w2t, *refs):
    *grads, send = refs
    half = rows // 2
    emit(flags, send, 0, w2t[j * half : (j + 1) * half] + both(s, m), grads)


def split(width):
    return width // 2 // 128 * 128


def packing(j, cut):
    head = slice(j * cut, (j + 1) * cut)
    return ((0, head), (1, head), (j, slice(2 * cut, None)))


def pack_body(cut, flags, *refs):
    pieces, outs = refs[:PARTS], refs[PARTS:]
    side = PARTS // 2
    for j, out in enumerate(outs):
        lane = 0
        for half, cols in packing(j, cut):
            row = 0
            for p in pieces[half * side : (half + 1) * side]:
                part = p[:, cols]
                out[row : row + part.shape[0], lane : lane + part.shape[1]] = part
                row += part.shape[0]
            lane += part.shape[1]


def upd2_next(j, cut, flags, s, m, w2t, s0, m0, s1, m1, colscale, *refs):
    *grads, send = refs
    half = s.shape[0]
    gain = colscale[...]
    moved = []
    for part, cols in packing(j, cut):
        sums, met = ((s0, m0), (s1, m1))[part]
        before = sums[:, cols].astype(F32) + met[:, cols].astype(F32)
        old = (w2t[part * half : (part + 1) * half, cols] + before) * gain[:, cols]
        moved.append(old + DECAY * before)
    emit(flags, send, 0, jnp.concatenate(moved, axis=1) + both(s, m), grads)


def column_scale(pieces, t2):
    sq = None
    count = 0
    for p in pieces:
        v = p[...].astype(F32)
        q = jnp.sum(v * v, axis=0, keepdims=True)
        sq = q if sq is None else sq + q
        count += p.shape[0]
    return t2 / jnp.sqrt(sq / count + EPS)


def scale_body(n_own, flags, *refs):
    pieces, t2, colscale, outs = refs[:-4], refs[-4], refs[-3], refs[-2:]
    sc = column_scale(pieces, t2[...])
    colscale[...] = sc
    for side in range(2):
        off = 0
        for p in pieces[side * n_own : (side + 1) * n_own]:
            n = p.shape[0]
            outs[side][off : off + n] = (p[...].astype(F32) * sc).astype(BF16)
            off += n


def hidden_body(block, flags, queries, *refs):
    *pieces, hidden, gate_rows, up_rows = refs
    part = pieces[0].shape[0] // 2
    for i, p in enumerate(pieces):
        gate_rows[i * part : (i + 1) * part] = p[:part]
        up_rows[i * part : (i + 1) * part] = p[part:]
    q = queries[block]
    gate = dot_nt(q, gate_rows[...])
    up = dot_nt(q, up_rows[...])
    _, act = silu_parts(gate)
    hidden[...] = (act * up).astype(BF16)


def pick_rows(flags, hidden, pick, n):
    if pick is None:
        return hidden[...]
    low, high = hidden[:n], hidden[n:]
    first, second = (low, high) if pick == 0 else (high, low)
    return jnp.where(is_set(flags, HEAD), second.astype(F32), first.astype(F32)).astype(BF16)


def out0_body(picks, flags, hidden, u2_own, u2_oth, *refs):
    *outs, stack = refs
    n = u2_own.shape[0]
    stack[:n] = u2_own[...]
    stack[n:] = u2_oth[...]
    for pick, out in zip(picks, outs):
        lhs = pick_rows(flags, hidden, pick, out.shape[0])
        out[...] = dot_nn(lhs, stack[...]).astype(BF16)


def out1_body(picks, which, cut, flags, hidden, a_own, a_oth, *refs):
    refs = list(refs)
    b_own, b_oth = (refs.pop(0), refs.pop(0)) if which else (None, None)
    t2, *outs, stack = refs
    half = a_own.shape[0]
    row = 0
    for a, b in ((a_own, b_own), (a_oth, b_oth)):
        for part in range(2):
            at = slice(row, row + half)
            src = b if which else a
            stack[at, :cut] = src[:, part * cut : (part + 1) * cut]
            if which:
                stack[at, cut:] = (a, b)[part][:, 2 * cut :]
            row += half
    rhs = stack[...]
    for pick, out in zip(picks, outs):
        res = dot_nn(pick_rows(flags, hidden, pick, out.shape[0]), rhs)
        cols = slice(cut, None) if which else slice(0, cut)
        out[...] = (res * column_scale((stack,), t2[:, cols])).astype(BF16)


def columns(flags, width, mine):
    head = flags[HEAD] if mine else 1 - flags[HEAD]
    return pl.multiple_of(head * width, 128)


def lay_body(width, cut, flags, own0, came0, own_a, own_b, came_a, out, sems):
    mine, other = columns(flags, width, True), columns(flags, width, False)
    for c in copies(
        sems,
        (own0, out.at[0, :, pl.ds(mine, width)]),
        (came0, out.at[0, :, pl.ds(other, width)]),
        (own_a, out.at[1, :, pl.ds(mine, cut)]),
        (own_b, out.at[1, :, pl.ds(mine + cut, width - cut)]),
        (came_a, out.at[1, :, pl.ds(other, cut)]),
    ):
        c.wait()


def fin_body(width, cut, rows, came_b, laid, out, sems):
    other = pl.multiple_of((1 - lax.axis_index("head")) * width, 128)
    for c in copies(sems, (came_b, out.at[1, :, pl.ds(other + cut, width - cut)])):
        c.wait()


def merged(pieces):
    return pieces[0] if len(pieces) == 1 else jnp.concatenate(pieces, axis=0)


PLAN = (
    (0, None), (1, None), (2, None), (3, 0), (4, 1), (5, 2), (None, 3), (6, 4),
    (7, 5), (8, None), (9, 6), (10, 7), (11, 8), (None, 9), (None, 10), (None, 11),
)


def local(queries, key_tokens, values, learn_rates, w_first, w_second, w_third):
    tok = lax.axis_size("tok")
    heads = lax.axis_size("head")
    cores = 2
    chips = tok // cores
    tokens, width = key_tokens.shape[1], key_tokens.shape[2]
    inner = w_first.shape[1]
    rows = inner // cores
    part = rows // PARTS
    half = rows // 2
    chunk = (half, width)
    grad_scale = 1.0 / math.sqrt(tokens * tok)
    lined = chips == 4
    tok_i = lax.axis_index("tok")
    chip_i = lax.div(tok_i, cores)
    outer = (chip_i == 0) | (chip_i == chips - 1) if lined else chip_i < 0
    place = jnp.stack(
        [lax.rem(tok_i, cores), outer.astype(jnp.int32), lax.axis_index("head")]
    ).astype(jnp.int32)
    flags = (place, jnp.broadcast_to(place[:, None], (3, width)))

    def shift(x, pairs):
        return lax.ppermute(x, "tok", pairs)

    def chip_pairs(to):
        return [(c * cores + i, to[c] * cores + i) for c in range(chips) for i in range(cores)]

    core_pairs = [(i, i ^ 1) for i in range(tok)]
    swap_ends = chip_pairs([1, 0, 3, 2]) if lined else None
    swap_mid = (
        [
            (i, j)
            for i, j in chip_pairs([0, 2, 1, 3])
            if i != j
        ]
        + [(i, j) for i, j in core_pairs if i // cores in (0, chips - 1)]
        if lined
        else None
    )

    full = (inner, width)
    mm = 2 * rows * width * tokens
    r_oth = shift(learn_rates, core_pairs)

    def loaded(b):
        k, v = call(
            functools.partial(load_body, b),
            flags,
            (key_tokens, values),
            [((tokens, width), BF16)] * 2,
            hbm=(0, 1),
            sems=2,
            grant=LOAD_GRANT[b],
        )
        return (k, shift(k, core_pairs), v, shift(v, core_pairs), learn_rates, r_oth)

    held = [loaded(b) for b in range(2)]
    k_own, k_oth, v_own, v_oth = held[0][:4]
    u13, w13, grads = [], [], {}
    for i in range(2):
        u, w, partial = call(
            functools.partial(first_body, False, i, grad_scale, rows),
            flags,
            (k_own, v_own, learn_rates, w_first, w_third),
            [((rows, width), BF16), ((rows, width), F32), ((half, width), F32)],
            3 * mm // 2,
            hbm=(3, 4),
            sems=2,
            grant=FIRST_GRANT,
            scalars=True,
        )
        u13.append(u)
        w13.append(w)
        grads[i] = call(
            functools.partial(first_body, True, i, grad_scale, rows),
            flags,
            (k_oth, v_oth, r_oth, u, partial),
            [(chunk, BF16)],
            3 * mm // 2,
        )
    w2t, u2t, t2 = call(
        functools.partial(flip_body, rows),
        flags,
        (w_second,),
        [((rows, width), F32), ((rows, width), BF16), ((1, width), F32)],
    )
    for i in range(2):
        chunk_grads = call(
            functools.partial(second_body, i, grad_scale),
            flags,
            (u13[i], u2t, *held[0]),
            [(chunk, BF16)] * (PARTS // 2),
            5 * mm,
        )
        for j, g in enumerate(chunk_grads):
            grads[2 + i * (PARTS // 2) + j] = [g]
    chunks = 2 * (PARTS + 2)
    finals, others, state = {}, {}, {}
    first13, next13, next2 = 2, PARTS + 2, 2 * PARTS + 2

    cut = split(width)
    seconds = []

    def gradient(j):
        g13, g2 = call(
            functools.partial(grad_body, j, grad_scale, 1),
            flags,
            (finals[first13 + j], state["u2_own"], *held[1]),
            [(chunk, BF16), ((part, width), BF16)],
            12 * mm // PARTS,
        )
        grads[next13 + j] = [g13]
        seconds.append(g2)
        if j == PARTS - 1:
            packed = call(
                functools.partial(pack_body, cut), flags, seconds, [(chunk, BF16)] * 2
            )
            for i, g in enumerate(packed):
                grads[next2 + i] = [g]

    def update(k, s, m, inw):
        state[k] = (s, m)
        side = PARTS // 2
        if k < first13:
            body, ins = functools.partial(upd2_first, k, rows), (w2t,)
        elif k < next13:
            j = k - first13
            body, ins = functools.partial(upd13_body, j % side), (w13[j // side],)
        elif k < next2:
            j = k - next13
            body = functools.partial(upd13_body, j % side)
            ins = (w13[j // side], *state[first13 + j])
        else:
            body = functools.partial(upd2_next, k - next2, cut)
            ins = (w2t, *state[0], *state[1], state["scale"])
        sums = grads[inw] if inw is not None else []
        (u,) = call(body, flags, (s, m, *ins, *sums), [(chunk, BF16)])
        return u

    def arrived(k):
        others[k] = shift(finals[k], core_pairs)
        if k == 1:
            state["scale"], state["u2_own"], state["u2_oth"] = call(
                functools.partial(scale_body, 2),
                flags,
                (finals[0], finals[1], others[0], others[1], t2),
                [((1, width), F32), ((rows, width), BF16), ((rows, width), BF16)],
            )

    def hidden_of(b, first):
        pieces = [finals[k] for k in first] + [others[k] for k in first]
        (hidden,) = call(
            functools.partial(hidden_body, b),
            flags,
            (queries, *pieces),
            [((tokens, inner), BF16)],
            8 * mm,
            scratch=[(full, BF16)] * 2,
        )
        return hidden

    def block0(picks, n):
        hidden = hidden_of(0, range(first13, next13))
        return call(
            functools.partial(out0_body, picks),
            flags,
            (hidden, state["u2_own"], state["u2_oth"]),
            [((n, width), BF16)] * len(picks),
            4 * mm,
            scratch=[(full, BF16)],
        )

    def block1(hidden, which, pick, n):
        ins = [hidden, finals[next2], others[next2]]
        if which:
            ins += [finals[next2 + 1], others[next2 + 1]]
        cols = width - cut if which else cut
        (res,) = call(
            functools.partial(out1_body, (pick,), which, cut),
            flags,
            (*ins, t2),
            [((n, cols), BF16)],
            2 * mm,
            scratch=[((inner, cols), BF16)],
        )
        return res

    def across(x):
        return lax.ppermute(x, "head", [(0, 1), (1, 0)])

    if lined:
        flight, sends = {}, {}
        for slot, (inw, out) in enumerate(PLAN):
            if inw is not None and inw not in grads:
                gradient(inw - next13)
            if out is not None:
                sends[slot] = update(out, *flight[out], inw)
            else:
                sends[slot] = merged(grads[inw])
            rcv = shift(sends[slot], swap_ends)
            if inw is not None:
                g = merged(grads[inw])
                total = (rcv.astype(F32) + g.astype(F32)).astype(BF16)
            if out is not None:
                finals[out] = jnp.where(outer, rcv, sends[slot])
            if inw is not None:
                flight[inw] = (total, shift(total, swap_mid))
            if out is not None:
                arrived(out)
    else:
        groups = [[c * cores + i for c in range(chips)] for i in range(cores)]
        zero = jnp.zeros(chunk, BF16)
        for k in range(chunks):
            if k not in grads:
                gradient(k - next13)
            s = lax.psum(merged(grads[k]), "tok", axis_index_groups=groups)
            finals[k] = update(k, s, zero, None)
            arrived(k)
    if heads != 2:
        (whole0,) = block0((None,), tokens)
        hidden = hidden_of(1, range(next13, next2))
        whole1 = jnp.concatenate(
            [block1(hidden, i, None, tokens) for i in range(2)], axis=1
        )
        return jnp.stack(
            [
                lax.all_to_all(x, "head", split_axis=0, concat_axis=1, tiled=True)
                for x in (whole0, whole1)
            ]
        )
    n = tokens // 2
    away, own0 = block0((1, 0), n)
    came0 = across(away)
    hidden = hidden_of(1, range(next13, next2))
    came_a = across(block1(hidden, 0, 1, n))
    came_b = across(block1(hidden, 1, 1, n))
    own_a = block1(hidden, 0, 0, n)
    own_b = block1(hidden, 1, 0, n)
    shape = [((2, n, 2 * width), BF16)]
    (laid,) = call(
        functools.partial(lay_body, width, cut),
        flags,
        (own0, came0, own_a, own_b, came_a),
        shape,
        out_hbm=True,
        sems=5,
        scalars=True,
    )
    (out,) = call(
        functools.partial(fin_body, width, cut),
        flags,
        (came_b, laid),
        shape,
        hbm=(1,),
        out_hbm=True,
        sems=1,
        alias={2: 0},
    )
    return out


def solution(mesh):
    placed = (
        P(None, ("grp", "tok"), "head"),
        P(None, ("grp", "tok"), "head"),
        P(None, ("grp", "tok"), "head"),
        P(None, "head", ("grp", "tok")),
        P("head", None, None),
        P("head", None, None),
        P("head", None, None),
    )
    return jax.shard_map(
        local,
        mesh=mesh,
        in_specs=placed,
        out_specs=P(None, ("grp", "tok", "head"), None),
        check_vma=False,
    )
```
